32 devices in a mesh: groups: 2 (over x), row: 16 (over z, y, core).
Axes of the slice: x: 2, y: 2, z: 4, core: 2. Of those that a mesh axis runs over, the one named last changes fastest.
Arguments:
- inverse: float32 [4, 4096, 4096], P('groups', 'row'), parts along dimension 0, as said below
- cycle: bfloat16 [4, 4096, 1024], P('groups', 'row'), parts along dimension 0, as said below
- arrivals: bfloat16 [4, 2, 4096, 128], P('groups', None, 'row'), parts along dimension 0, may hold values from -6 to 6
- departing: int32 [4, 128], P('groups'), parts along dimension 0, may hold values from 0 to 1023, as said below
- directions: int32 [4, 512], P('groups'), parts along dimension 0, may hold values from 0 to 8191
Outputs:
- new_inverse: float32 [4, 4096, 4096], P('groups', 'row'), parts along dimension 0
- beam_weights: float32 [4, 2, 4096, 512], P('groups', None, 'row'), parts along dimension 0
- spectrum: float32 [4, 512], P('groups'), parts along dimension 0
The draws below stay inside these ranges and needn't reach their ends.
There are 2 independent parts, one for each index of `groups`. The reference program is written for one: setup_inputs(seed, part) draws one part's arguments, and reference() takes and returns one part's arrays. A program takes and returns all parts, laid end to end along the dimension named above; each array names one. Nothing has to cross between parts.
Inputs may be any that keep to these rules, and one draw needn't show every extreme that they name: inverse is Hermitian and is the inverse of I + cycle cycle^H / 1024. `cycle`: the snapshots whose inverse covariance is given. `departing`: all 2 x 128 entries are different slots.
All inputs are finite; a program needn't handle non-finite values.
Results may differ from the reference program's by a relative error of at most 0.0003.
Values may be sent and summed in bfloat16 or wider, within the bound.
No kernel may reach another device: no remote copies, remote signals or barrier semaphores. Data moves between devices by JAX's collectives and lax.ppermute only.
A program may use at most 192 MiB of HBM per device.

```python
import jax
import jax.numpy as jnp
from jax import lax

M = 4096
SNAP = 128
CYCLE = 1024
STEPS = 2
DIRS = 512
ANGLES = 8192


def window_snapshots(key):
    base = jax.random.fold_in(key, 7)
    values = jax.random.normal(base, (2, M, CYCLE), jnp.float32)
    return values.astype(jnp.bfloat16)


def draw_cycle(key, part):
    return window_snapshots(key)


def draw_inverse(key, part):
    snaps = window_snapshots(key).astype(jnp.float32)
    snap_re, snap_im = (snaps[0], snaps[1])
    hp = lax.Precision.HIGHEST
    gram_re = jnp.dot(snap_re.T, snap_re, precision=hp) + jnp.dot(snap_im.T, snap_im, precision=hp)
    gram_im = jnp.dot(snap_re.T, snap_im, precision=hp) - jnp.dot(snap_im.T, snap_re, precision=hp)
    gram_re = gram_re + CYCLE * jnp.eye(CYCLE, dtype=jnp.float32)
    embedded = jnp.concatenate([jnp.concatenate([gram_re, -gram_im], 1), jnp.concatenate([gram_im, gram_re], 1)], 0)
    rhs = jnp.concatenate([snap_re.T, -snap_im.T], 0)
    solution = jnp.linalg.solve(embedded, rhs)
    sol_re, sol_im = (solution[:CYCLE], solution[CYCLE:])
    prod_re = jnp.dot(snap_re, sol_re, precision=hp) - jnp.dot(snap_im, sol_im, precision=hp)
    prod_im = jnp.dot(snap_re, sol_im, precision=hp) + jnp.dot(snap_im, sol_re, precision=hp)
    inv_re = jnp.eye(M, dtype=jnp.float32) - prod_re
    inv_im = -prod_im
    inv_re = 0.5 * (inv_re + inv_re.T)
    inv_im = 0.5 * (inv_im - inv_im.T)
    return jnp.stack([inv_re, inv_im]).astype(jnp.float32)


def draw_departing(key, part):
    total = STEPS * SNAP
    others = jax.random.permutation(jax.random.fold_in(key, 11), CYCLE - 1)[:total - 1]
    chosen = jnp.concatenate([others.astype(jnp.int32), jnp.full((1,), CYCLE - 1, jnp.int32)])
    mixed = jax.random.permutation(jax.random.fold_in(key, 13), chosen)
    return mixed.reshape(STEPS, SNAP).astype(jnp.int32)


def set_ends(entries, key, smallest, top_value):
    spot = [jax.random.randint(jax.random.fold_in(key, axis), (), 0, length) for axis, length in enumerate(entries.shape)]
    main_axis = entries.shape.index(max(entries.shape))
    neighbour = spot[:main_axis] + [(spot[main_axis] + 1) % entries.shape[main_axis]] + spot[main_axis + 1:]
    return entries.at[tuple(spot)].set(smallest).at[tuple(neighbour)].set(top_value)


def shard_levels(rng, dims, pieces, low, high):
    def one(axis_at, shards_of):
        draws = jax.random.uniform(jax.random.fold_in(jax.random.fold_in(rng, 6), axis_at), (shards_of,), jnp.float32, low / len(pieces), high / len(pieces))
        return jnp.repeat(jnp.exp(draws), dims[axis_at] // shards_of).reshape((-1,) + (1,) * (len(dims) - axis_at - 1))

    gain = one(*pieces[0])
    for cut in pieces[1:]:
        gain = gain * one(*cut)
    return gain


def noise(rng, extent, deviation, most, split=(), kind=jnp.bfloat16):
    result = deviation * jax.random.normal(rng, extent, jnp.float32)
    if split:
        result = result * shard_levels(rng, extent, split, -0.22, 0.18)
    return jnp.clip(result, -most, most).astype(kind)


def setup_inputs(seed: int = 0, part: int = 0) -> dict:
    key_list = jax.random.split(jax.random.key(seed), 6)
    part_keys = jax.random.split(jax.random.fold_in(key_list[5], part), 6)
    return {
        "inverse": draw_inverse(jax.random.fold_in(jax.random.fold_in(key_list[5], part), 71), part),
        "cycle": draw_cycle(jax.random.fold_in(jax.random.fold_in(key_list[5], part), 71), part),
        "arrivals": noise(part_keys[2], (STEPS, 2, M, SNAP), 1.0, 6.0, ((2, 16),)),
        "departing": draw_departing(jax.random.fold_in(jax.random.fold_in(key_list[5], part), 71), part),
        "directions": set_ends(jax.random.randint(part_keys[4], (STEPS, DIRS), 0, ANGLES), jax.random.fold_in(part_keys[4], 1), 0, ANGLES - 1).astype(jnp.int32),
    }


precise = lax.Precision.HIGHEST

def matmul(left, right):
    return jnp.dot(left.astype(jnp.float32), right.astype(jnp.float32), precision=precise, preferred_element_type=jnp.float32)

def lead_dot(left, right):
    return lax.dot_general(left.astype(jnp.float32), right.astype(jnp.float32), (((0,), (0,)), ((), ())), precision=precise, preferred_element_type=jnp.float32)

def steering(direction_ids, length):
    element = jnp.arange(length, dtype=jnp.int32)[:, None]
    odd_index = 2 * direction_ids[None, :] + 1
    angle_count = 2 * length
    turns = (element * odd_index - element * angle_count) % (2 * angle_count)
    phase = jnp.pi * turns.astype(jnp.float32) / angle_count
    return (jnp.cos(phase), jnp.sin(phase))

def reference(inverse, cycle, arrivals, departing, directions):
    inv_re, inv_im = (inverse[0], inverse[1])
    weight_list = []
    power_list = []
    for step_index in range(STEPS):
        steer_re, steer_im = steering(directions[step_index], M)
        app_re = matmul(inv_re, steer_re) - matmul(inv_im, steer_im)
        app_im = matmul(inv_re, steer_im) + matmul(inv_im, steer_re)
        power = jnp.sum(steer_re * app_re + steer_im * app_im, axis=0)
        weight_list.append(jnp.stack([M * app_re / power, M * app_im / power]))
        power_list.append(M / power)
        departed = jnp.take(cycle, departing[step_index], axis=2)
        snap_wide = jnp.concatenate([arrivals[step_index], departed], axis=2).astype(jnp.float32)
        q_re = matmul(inv_re, snap_wide[0]) - matmul(inv_im, snap_wide[1])
        q_im = matmul(inv_re, snap_wide[1]) + matmul(inv_im, snap_wide[0])
        cap_re = lead_dot(snap_wide[0], q_re) + lead_dot(snap_wide[1], q_im)
        cap_im = lead_dot(snap_wide[0], q_im) - lead_dot(snap_wide[1], q_re)
        signs = jnp.concatenate([jnp.ones((SNAP,), jnp.float32), -jnp.ones((SNAP,), jnp.float32)])
        g_re = CYCLE * jnp.diag(signs) + cap_re
        g_im = cap_im
        embedded = jnp.concatenate([jnp.concatenate([g_re, -g_im], 1), jnp.concatenate([g_im, g_re], 1)], 0)
        rhs = jnp.concatenate([q_re.T, -q_im.T], 0)
        solution = jnp.linalg.solve(embedded, rhs)
        half = 2 * SNAP
        x_re, x_im = (solution[:half], solution[half:])
        inv_re = inv_re - (matmul(q_re, x_re) - matmul(q_im, x_im))
        inv_im = inv_im - (matmul(q_re, x_im) + matmul(q_im, x_re))
    return (jnp.stack([inv_re, inv_im]), jnp.stack(weight_list), jnp.stack(power_list))
```

```python
import jax
import jax.numpy as jnp
from jax import lax
from jax.experimental import pallas as pl
from jax.experimental.pallas import tpu as pltpu
from jax.sharding import PartitionSpec as P

STEPS = 2

f32 = jnp.float32
bf16 = jnp.bfloat16
HIGHEST = lax.Precision.HIGHEST
LANES = 128


def split(x):
    high = x.astype(bf16)
    return high, (x - high.astype(f32)).astype(bf16)


def mm(left, right):
    return jnp.dot(left, right, preferred_element_type=f32)


def mm_tn(left, right):
    return lax.dot_general(left, right, (((0,), (0,)), ((), ())), preferred_element_type=f32)


def mm_nt(left, right):
    return lax.dot_general(left, right, (((1,), (1,)), ((), ())), preferred_element_type=f32)


def exact(left, right, dims=((1,), (0,))):
    return lax.dot_general(left, right, (dims, ((), ())), precision=HIGHEST, preferred_element_type=f32)


def ring_order(row_count):
    chips = row_count // 2
    return list(range(0, chips, 2)) + list(reversed(range(1, chips, 2)))


def ring_perm(row_count, shift):
    order = ring_order(row_count)
    chips = len(order)
    return [
        (order[i] * 2 + core, order[(i + shift) % chips] * 2 + core) for i in range(chips) for core in range(2)
    ]


def ring_gather(block, row_count):
    chips = row_count // 2
    right_count = chips // 2
    left_count = chips - 1 - right_count
    right = left = block
    swap = [(i, i ^ 1) for i in range(row_count)]
    groups = [[block, lax.ppermute(block, "row", swap)]]
    for hop in range(1, right_count + 1):
        right = lax.ppermute(right, "row", ring_perm(row_count, 1))
        group = [right]
        if hop <= left_count:
            left = lax.ppermute(left, "row", ring_perm(row_count, -1))
            group.append(left)
        groups.append(group + [lax.ppermute(x, "row", swap) for x in group])
    return groups


def ring_sources(row_count):
    order = ring_order(row_count)
    chips = len(order)
    position = [0] * chips
    for place, chip in enumerate(order):
        position[chip] = place
    me = lax.axis_index("row")
    core = me % 2
    here = jnp.asarray(position, jnp.int32)[me // 2]
    table = jnp.asarray(order, jnp.int32)
    right_count = chips // 2
    left_count = chips - 1 - right_count
    groups = [jnp.stack([me, me ^ 1]).astype(jnp.int32)]
    for hop in range(1, right_count + 1):
        chip = [table[(here - hop) % chips]]
        if hop <= left_count:
            chip.append(table[(here + hop) % chips])
        groups.append(jnp.stack([c * 2 + core for c in chip] + [c * 2 + 1 - core for c in chip]).astype(jnp.int32))
    return groups


def tree_sum(x, row_count):
    if row_count & (row_count - 1):
        return lax.psum(x, "row")
    step = 1
    while step < row_count:
        x = x + lax.ppermute(x, "row", [(i, i ^ step) for i in range(row_count)])
        step *= 2
    return x


def steering_tables(directions, length, inner):
    odd = 2 * directions[None, :] + 1 - 2 * length

    def table(elements):
        turns = (elements[:, None] * odd) % (4 * length)
        phase = jnp.pi * turns.astype(f32) / (2 * length)
        return jnp.stack([jnp.cos(phase), jnp.sin(phase)])

    coarse = table(jnp.arange(length // inner, dtype=jnp.int32) * inner)
    fine = table(jnp.arange(inner, dtype=jnp.int32))
    return coarse, fine


def steer_rows(coarse_ref, fine_ref, index):
    er, ei = coarse_ref[0, pl.ds(index, 1), :], coarse_ref[1, pl.ds(index, 1), :]
    fr, fi = fine_ref[0], fine_ref[1]
    return er * fr - ei * fi, er * fi + ei * fr


def steer_kernel(first_ref, p_ref, coarse_ref, fine_ref, h_ref, power_ref, acc, a_high, a_low):
    step = pl.program_id(0)
    rows, width = p_ref.shape[1], p_ref.shape[2]
    inner, dirs = fine_ref.shape[1], fine_ref.shape[2]
    count = width // inner
    for a in range(count):
        ar, ai = steer_rows(coarse_ref, fine_ref, step * count + a)
        place = slice(a * inner, (a + 1) * inner)
        a_high[place, :dirs], a_low[place, :dirs] = split(ar)
        a_high[place, dirs:], a_low[place, dirs:] = split(ai)
    p_high, p_low = split(p_ref[...].reshape(2 * rows, width))
    part = mm(p_high, a_high[...]) + mm(p_low, a_high[...]) + mm(p_high, a_low[...])

    @pl.when(step == 0)
    def _():
        acc[...] = part

    @pl.when(step > 0)
    def _():
        acc[...] += part

    @pl.when(step == pl.num_programs(0) - 1)
    def _():
        h_re = acc[:rows, :dirs] - acc[rows:, dirs:]
        h_im = acc[:rows, dirs:] + acc[rows:, :dirs]
        h_ref[0], h_ref[1] = h_re, h_im
        power = jnp.zeros((1, dirs), f32)
        for a in range(rows // inner):
            ar, ai = steer_rows(coarse_ref, fine_ref, first_ref[0] + a)
            place = slice(a * inner, (a + 1) * inner)
            power += jnp.sum(ar * h_re[place] + ai * h_im[place], axis=0, keepdims=True)
        power_ref[...] = power


def steer_product(inverse, coarse, fine, first):
    _, rows, length = inverse.shape
    dirs = coarse.shape[2]
    width = min(512, length)
    return pl.pallas_call(
        steer_kernel,
        grid_spec=pltpu.PrefetchScalarGridSpec(
            num_scalar_prefetch=1,
            grid=(length // width,),
            in_specs=[
                pl.BlockSpec((2, rows, width), lambda k, s: (0, 0, k)),
                pl.BlockSpec(coarse.shape, lambda k, s: (0, 0, 0)),
                pl.BlockSpec(fine.shape, lambda k, s: (0, 0, 0)),
            ],
            out_specs=[
                pl.BlockSpec((2, rows, dirs), lambda k, s: (0, 0, 0)),
                pl.BlockSpec((1, dirs), lambda k, s: (0, 0)),
            ],
            scratch_shapes=[
                pltpu.VMEM((2 * rows, 2 * dirs), f32),
                pltpu.VMEM((width, 2 * dirs), bf16),
                pltpu.VMEM((width, 2 * dirs), bf16),
            ],
        ),
        out_shape=[jax.ShapeDtypeStruct((2, rows, dirs), f32), jax.ShapeDtypeStruct((1, dirs), f32)],
        name="steer",
    )(first, inverse, coarse, fine)


def snap_kernel(count, has_acc, is_last, _, *refs):
    p_refs, u_refs = refs[:count], refs[count : 2 * count]
    rest = refs[2 * count :]
    out_ref = rest[-1]
    rows = p_refs[0].shape[1]
    acc = rest[0][...] if has_acc else None
    for p_ref, u_ref in zip(p_refs, u_refs):
        p_high, p_low = split(p_ref[...].reshape(2 * rows, p_ref.shape[2]))
        snaps = u_ref[...]
        part = mm(p_high, snaps) + mm(p_low, snaps)
        acc = part if acc is None else acc + part
    if is_last:
        for start in range(0, acc.shape[1], 2 * LANES):
            re, im = slice(start, start + LANES), slice(start + LANES, start + 2 * LANES)
            out_ref[:, re] = acc[:rows, re] + acc[rows:, im]
            out_ref[:, im] = acc[:rows, im] - acc[rows:, re]
    else:
        out_ref[...] = acc


def snap_product(inverse, snaps, sources, acc, is_last):
    _, rows, _ = inverse.shape
    width = snaps[0].shape[1]
    count = len(snaps)
    whole = lambda *_: (0, 0)
    specs = [pl.BlockSpec((2, rows, rows), lambda i, s, g=g: (0, 0, s[g])) for g in range(count)]
    specs += [pl.BlockSpec((rows, width), whole)] * count
    args = [inverse] * count + snaps
    if acc is not None:
        specs.append(pl.BlockSpec((2 * rows, width), whole))
        args.append(acc)
    out_rows = rows if is_last else 2 * rows
    return pl.pallas_call(
        lambda *refs: snap_kernel(count, acc is not None, is_last, *refs),
        grid_spec=pltpu.PrefetchScalarGridSpec(
            num_scalar_prefetch=1,
            grid=(1,),
            in_specs=specs,
            out_specs=pl.BlockSpec((out_rows, width), whole),
        ),
        out_shape=jax.ShapeDtypeStruct((out_rows, width), f32),
        name="snaps",
    )(sources, *args)


def cross_kernel(count, has_acc, src_ref, coarse_ref, fine_ref, *refs):
    u_refs, q_refs = refs[:count], refs[count : 2 * count]
    rest = refs[2 * count :]
    k_ref, b_ref = rest[-4], rest[-3]
    a_high, a_low = rest[-2], rest[-1]
    rows, width = u_refs[0].shape
    half = width // 2
    block = 2 * LANES
    inner, dirs = fine_ref.shape[1], fine_ref.shape[2]
    for g in range(count):
        for a in range(rows // inner):
            ar, ai = steer_rows(coarse_ref, fine_ref, src_ref[g] * (rows // inner) + a)
            place = slice(a * inner, (a + 1) * inner)
            a_high[place, :dirs], a_low[place, :dirs] = split(ar)
            a_high[place, dirs:], a_low[place, dirs:] = split(ai)
        q_high, q_low = split(q_refs[g][...])
        first_h, first_l = q_high[:, :half], q_low[:, :half]
        part = mm_tn(first_h, a_high[...]) + mm_tn(first_l, a_high[...]) + mm_tn(first_h, a_low[...])
        if g == 0:
            b_ref[...] = part + rest[1][...] if has_acc else part
        else:
            b_ref[...] += part
        for q in range(0, width, block):
            left = u_refs[g][:, q:]
            part = mm_tn(left, q_high[:, q : q + block]) + mm_tn(left, q_low[:, q : q + block])
            if g == 0:
                k_ref[q:, q : q + block] = part + rest[0][q:, q : q + block] if has_acc else part
            else:
                k_ref[q:, q : q + block] += part


def cross_products(snaps, products, sources, coarse, fine, acc):
    rows, width = snaps[0].shape
    count = len(snaps)
    dirs = coarse.shape[2]
    whole = lambda *_: (0, 0)
    shapes = [(width, width), (width // 2, 2 * dirs)]
    specs = [pl.BlockSpec(coarse.shape, lambda *_: (0, 0, 0)), pl.BlockSpec(fine.shape, lambda *_: (0, 0, 0))]
    specs += [pl.BlockSpec((rows, width), whole)] * (2 * count)
    args = [coarse, fine] + snaps + products
    if acc is not None:
        specs += [pl.BlockSpec(s, whole) for s in shapes]
        args += list(acc)
    return pl.pallas_call(
        lambda *refs: cross_kernel(count, acc is not None, *refs),
        grid_spec=pltpu.PrefetchScalarGridSpec(
            num_scalar_prefetch=1,
            grid=(1,),
            in_specs=specs,
            out_specs=[pl.BlockSpec(s, whole) for s in shapes],
            scratch_shapes=[pltpu.VMEM((rows, 2 * dirs), bf16), pltpu.VMEM((rows, 2 * dirs), bf16)],
        ),
        out_shape=[jax.ShapeDtypeStruct(s, f32) for s in shapes],
        name="cross",
    )(sources, *args)


def eye(n):
    return (lax.broadcasted_iota(jnp.int32, (n, n), 0) == lax.broadcasted_iota(jnp.int32, (n, n), 1)).astype(f32)


def spd_inverse(matrix):
    n = matrix.shape[0]
    ident = eye(n)
    norm = jnp.max(jnp.sum(jnp.abs(matrix), axis=0, keepdims=True))
    start = ident * (1.9 / norm)

    def residual(x):
        r = ident - exact(matrix, x)
        return r, jnp.sum(r * r)

    def cond(state):
        _, _, size, last, count = state
        return jnp.logical_and(count < 64, jnp.logical_or(size > 0.25, jnp.logical_and(size > 1e-9, size < 0.5 * last)))

    def body(state):
        x, r, size, _, count = state
        x = x + exact(x, r)
        r, new_size = residual(x)
        return x, r, new_size, size, count + 1

    r, size = residual(start)
    x, r, _, _, _ = lax.while_loop(cond, body, (start, r, size, size * 4.0, 0))
    x = x + exact(x, r)
    return 0.5 * (x + x.T)


def quasi_inverse(e00, e10, e11):
    first = spd_inverse(e00)
    v = exact(first, e10, ((1,), (1,)))
    schur = e11 - exact(e10, v)
    second = -spd_inverse(-0.5 * (schur + schur.T))
    cross = exact(v, second)
    corner = first + exact(cross, v, ((1,), (1,)))
    top = jnp.concatenate([corner, -cross], 1)
    return jnp.concatenate([top, jnp.concatenate([-cross.T, second], 1)], 0)


def solve_kernel(window, k_ref, b_ref, q_ref, h_ref, x_ref, h_out, power_ref):
    block = 2 * LANES
    width = k_ref.shape[0]
    half = width // 2

    def embedded(p, q):
        m = k_ref[p * block : (p + 1) * block, q * block : (q + 1) * block]
        re = m[:LANES, :LANES] + m[LANES:, LANES:]
        im = m[LANES:, :LANES] - m[:LANES, LANES:]
        e = jnp.concatenate([jnp.concatenate([re, -im], 1), jnp.concatenate([im, re], 1)], 0)
        if p != q:
            return e
        sign = 1.0 if p % 2 == 0 else -1.0
        return 0.5 * (e + e.T) + (sign * window) * eye(block)

    inv1 = quasi_inverse(embedded(0, 0), embedded(1, 0), embedded(1, 1))
    k21 = jnp.concatenate(
        [jnp.concatenate([embedded(2, 0), embedded(2, 1)], 1), jnp.concatenate([embedded(3, 0), embedded(3, 1)], 1)], 0
    )
    w = exact(inv1, k21, ((1,), (1,)))
    fold = exact(k21, w)
    g00 = embedded(2, 2) - fold[:block, :block]
    g10 = embedded(3, 2) - fold[block:, :block]
    g11 = embedded(3, 3) - fold[block:, block:]
    inv2 = quasi_inverse(0.5 * (g00 + g00.T), g10, 0.5 * (g11 + g11.T))
    q1, q2 = q_ref[:, :half], q_ref[:, half:]
    y = exact(q1, inv1)
    x2 = exact(q2 - exact(q1, w), inv2)
    x_ref[:, half:] = x2
    x_ref[:, :half] = y - exact(x2, w, ((1,), (1,)))
    dirs = h_ref.shape[2]
    res, ims = [], []
    for start in range(0, half, block):
        top, low = slice(start, start + LANES), slice(start + LANES, start + block)
        re = b_ref[top, :dirs] - b_ref[low, dirs:]
        im = b_ref[top, dirs:] + b_ref[low, :dirs]
        res += [re, im]
        ims += [im, -re]
    b_re, b_im = jnp.concatenate(res, 0), jnp.concatenate(ims, 0)
    h_out[0] = h_ref[0] - exact(y, b_re)
    h_out[1] = h_ref[1] - exact(y, b_im)
    power_ref[...] = jnp.sum(b_re * exact(inv1, b_re), axis=0, keepdims=True)


def solve(window, kmat, bmat, local, h):
    width = kmat.shape[0]
    rows, dirs = h.shape[1], h.shape[2]
    return pl.pallas_call(
        lambda *refs: solve_kernel(window, *refs),
        out_shape=[
            jax.ShapeDtypeStruct((rows, width), f32),
            jax.ShapeDtypeStruct(h.shape, f32),
            jax.ShapeDtypeStruct((1, dirs), f32),
        ],
        name="solve",
    )(kmat, bmat, local, h)


def update_kernel(count, src_ref, p_ref, x_ref, *refs):
    q_refs = refs[:count]
    out_ref, buf, sem = refs[count:]
    step = pl.program_id(0)

    def copy(g, slot):
        return pltpu.make_async_copy(q_refs[g], buf.at[slot], sem.at[slot])

    @pl.when(step == 0)
    def _():
        copy(0, 0).start()

    for g in range(1, count):

        @pl.when(step + 1 == g)
        def _(g=g):
            copy(g, g % 2).start()

    slot = step % 2
    copy(0, slot).wait()
    rows = p_ref.shape[1]
    x_high, x_low = split(x_ref[...])
    q = buf[slot]
    width = q.shape[1]
    q_high, q_low = split(q)

    def turned(v):
        parts = []
        for start in range(0, width, 2 * LANES):
            parts += [-v[:, start + LANES : start + 2 * LANES], v[:, start : start + LANES]]
        return jnp.concatenate(parts, 1)

    out_ref[0] = p_ref[0] - (mm_nt(x_high, q_high) + mm_nt(x_low, q_high) + mm_nt(x_high, q_low))
    t_high, t_low = turned(q_high), turned(q_low)
    out_ref[1] = p_ref[1] + (mm_nt(x_high, t_high) + mm_nt(x_low, t_high) + mm_nt(x_high, t_low))


def update(inverse, x, products, sources):
    _, rows, length = inverse.shape
    width = x.shape[1]
    count = len(products)
    return pl.pallas_call(
        lambda *refs: update_kernel(count, *refs),
        grid_spec=pltpu.PrefetchScalarGridSpec(
            num_scalar_prefetch=1,
            grid=(count,),
            in_specs=[
                pl.BlockSpec((2, rows, rows), lambda i, s: (0, 0, s[i])),
                pl.BlockSpec((rows, width), lambda i, s: (0, 0)),
            ]
            + [pl.BlockSpec(memory_space=pl.ANY)] * count,
            out_specs=pl.BlockSpec((2, rows, rows), lambda i, s: (0, 0, s[i])),
            scratch_shapes=[pltpu.VMEM((2, rows, width), f32), pltpu.SemaphoreType.DMA((2,))],
        ),
        out_shape=jax.ShapeDtypeStruct(inverse.shape, f32),
        name="update",
    )(sources, inverse, x, *products)


def on_device(row_count, inverse, cycle, arrivals, departing, directions):
    rows, length = inverse.shape[1], inverse.shape[2]
    window = cycle.shape[2]
    snap = arrivals.shape[3]
    dirs = directions.shape[1]
    inner = 64
    first = (lax.axis_index("row") * (rows // inner)).astype(jnp.int32)[None]

    slots = departing.reshape(-1)
    pick = (jnp.arange(window, dtype=jnp.int32)[:, None] == slots[None, :]).astype(bf16)
    departed = mm(cycle.reshape(2 * rows, window), pick).astype(bf16).reshape(2, rows, -1)
    blocks = []
    for t in range(STEPS):
        gone = departed[:, :, t * snap : (t + 1) * snap]
        blocks += [arrivals[t, 0], -arrivals[t, 1], gone[0], -gone[1]]
    own = jnp.concatenate(blocks, 1)
    snap_groups = ring_gather(own, row_count)
    sources = ring_sources(row_count)

    tables = [steering_tables(directions[t], length, inner) for t in range(STEPS)]
    part = dirs // 2
    steered, powers = [], []
    for t in range(STEPS):
        coarse, fine = tables[t]
        halves = [
            steer_product(inverse, coarse[:, :, s : s + part], fine[:, :, s : s + part], first)
            for s in range(0, dirs, part)
        ]
        steered.append(jnp.concatenate([h for h, _ in halves], 2))
        powers += [p for _, p in halves]
    power = tree_sum(jnp.concatenate(powers, 0), row_count).reshape(STEPS, dirs)

    acc = None
    for hop, group in enumerate(snap_groups):
        acc = snap_product(inverse, group, sources[hop], acc, hop == len(snap_groups) - 1)
    local = acc
    product_groups = ring_gather(local.astype(jnp.float16), row_count)
    product_groups = [[q.astype(f32) for q in group] for group in product_groups]

    coarse, fine = tables[1]
    acc = None
    for some in ((0, 1), (2, 3), tuple(range(4, len(snap_groups)))):
        some = [s for s in some if s < len(snap_groups)]
        if not some:
            continue
        snaps = [u for s in some for u in snap_groups[s]]
        products = [q for s in some for q in product_groups[s]]
        acc = cross_products(snaps, products, jnp.concatenate([sources[s] for s in some]), coarse, fine, acc)
    kmat, bmat = acc

    x, second, fold = solve(float(window), kmat, bmat, local, steered[1])
    power = jnp.concatenate([power[:1], power[1:] - fold], 0)
    new_inverse = update(
        inverse, x, [q for group in product_groups for q in group], jnp.concatenate(sources)
    )
    spectrum = length / power
    weights = jnp.stack([steered[0] * spectrum[0], second * spectrum[1]])
    return new_inverse, weights, spectrum


def solution(mesh):
    row_count = mesh.shape["row"]
    in_specs = (
        P("groups", "row", None),
        P("groups", "row", None),
        P("groups", None, "row", None),
        P("groups", None),
        P("groups", None),
    )
    out_specs = (P("groups", "row", None), P("groups", None, "row", None), P("groups", None))
    return jax.shard_map(
        lambda *args: on_device(row_count, *args), mesh=mesh, in_specs=in_specs, out_specs=out_specs, check_vma=False
    )
```

```python
import jax
import jax.numpy as jnp
from jax import lax
from jax.experimental import pallas as pl
from jax.experimental.pallas import tpu as pltpu
from jax.sharding import PartitionSpec as P

STEPS = 2

f32 = jnp.float32
bf16 = jnp.bfloat16
HIGHEST = lax.Precision.HIGHEST
LANES = 128


def split(x):
    high = x.astype(bf16)
    return high, (x - high.astype(f32)).astype(bf16)


def mm(left, right):
    return jnp.dot(left, right, preferred_element_type=f32)


def mm_tn(left, right):
    return lax.dot_general(left, right, (((0,), (0,)), ((), ())), preferred_element_type=f32)


def mm_nt(left, right):
    return lax.dot_general(left, right, (((1,), (1,)), ((), ())), preferred_element_type=f32)


def exact(left, right, dims=((1,), (0,))):
    return lax.dot_general(left, right, (dims, ((), ())), precision=HIGHEST, preferred_element_type=f32)


def ring_order(row_count):
    chips = row_count // 2
    return list(range(0, chips, 2)) + list(reversed(range(1, chips, 2)))


def hop(block, row_count, shift):
    order = ring_order(row_count)
    chips = len(order)
    pairs = [(order[i] * 2 + core, order[(i + shift) % chips] * 2 + core) for i in range(chips) for core in range(2)]
    return lax.ppermute(block, "row", pairs)


def swap(block, row_count):
    return lax.ppermute(block, "row", [(i, i ^ 1) for i in range(row_count)])


def ring_counts(row_count):
    chips = row_count // 2
    right = chips // 2
    return right, chips - 1 - right


def together(*trees):
    return lax.optimization_barrier(trees)


def ring_sources(row_count):
    order = ring_order(row_count)
    chips = len(order)
    position = [0] * chips
    for place, chip in enumerate(order):
        position[chip] = place
    me = lax.axis_index("row")
    core = me % 2
    here = jnp.asarray(position, jnp.int32)[me // 2]
    right, left = ring_counts(row_count)
    shifts = [[0]] + [[-h, h] if h <= left else [-h] for h in range(1, right + 1)]
    flat = jnp.asarray([s for group in shifts for s in group], jnp.int32)
    chip = jnp.asarray(order, jnp.int32)[(here + flat) % chips]
    mine, theirs = (chip * 2 + core).astype(jnp.int32), (chip * 2 + 1 - core).astype(jnp.int32)
    groups, at = [], 0
    for group in shifts:
        groups.append((mine[at : at + len(group)], theirs[at : at + len(group)]))
        at += len(group)
    return groups


def tree_sum(x, row_count):
    if row_count & (row_count - 1):
        return lax.psum(x, "row")
    step = 1
    while step < row_count:
        x = x + lax.ppermute(x, "row", [(i, i ^ step) for i in range(row_count)])
        step *= 2
    return x


def steering_tables(directions, length, inner):
    odd = 2 * directions[None, :] + 1 - 2 * length

    def table(elements):
        turns = (elements[:, None] * odd) % (4 * length)
        phase = jnp.pi * turns.astype(f32) / (2 * length)
        return jnp.stack([jnp.cos(phase), jnp.sin(phase)])

    coarse = table(jnp.arange(length // inner, dtype=jnp.int32) * inner)
    fine = table(jnp.arange(inner, dtype=jnp.int32))
    return coarse, fine


def steer_rows(coarse_ref, fine_ref, index):
    er, ei = coarse_ref[0, pl.ds(index, 1), :], coarse_ref[1, pl.ds(index, 1), :]
    fr, fi = fine_ref[0], fine_ref[1]
    return er * fr - ei * fi, er * fi + ei * fr


def embed(re, im):
    return jnp.concatenate([jnp.concatenate([re, -im], 1), jnp.concatenate([im, re], 1)], 0)


def steer_kernel(first_ref, p_ref, coarse_ref, fine_ref, h_ref, power_ref, acc, a_high, a_low):
    step = pl.program_id(0)
    rows, width = p_ref.shape[1], p_ref.shape[2]
    inner, dirs = fine_ref.shape[1], fine_ref.shape[2]
    count = width // inner
    for a in range(count):
        ar, ai = steer_rows(coarse_ref, fine_ref, step * count + a)
        top, low = slice(a * inner, (a + 1) * inner), slice(width + a * inner, width + (a + 1) * inner)
        a_high[top, :], a_low[top, :] = split(ar)
        a_high[low, :], a_low[low, :] = split(ai)
    re_high, re_low = split(p_ref[0])
    im_high, im_low = split(p_ref[1])
    high = embed(re_high, im_high)
    part = mm(high, a_high[...]) + mm(embed(re_low, im_low), a_high[...]) + mm(high, a_low[...])

    @pl.when(step == 0)
    def _():
        acc[...] = part

    @pl.when(step > 0)
    def _():
        acc[...] += part

    @pl.when(step == pl.num_programs(0) - 1)
    def _():
        h_ref[0], h_ref[1] = acc[:rows, :], acc[rows:, :]
        power = jnp.zeros((1, dirs), f32)
        for a in range(rows // inner):
            ar, ai = steer_rows(coarse_ref, fine_ref, first_ref[0] + a)
            place = slice(a * inner, (a + 1) * inner)
            power += jnp.sum(ar * h_ref[0, place] + ai * h_ref[1, place], axis=0, keepdims=True)
        power_ref[...] = power


def steer_product(inverse, coarse, fine, first):
    _, rows, length = inverse.shape
    dirs = coarse.shape[2]
    width = min(512, length)
    return pl.pallas_call(
        steer_kernel,
        grid_spec=pltpu.PrefetchScalarGridSpec(
            num_scalar_prefetch=1,
            grid=(length // width,),
            in_specs=[
                pl.BlockSpec((2, rows, width), lambda k, s: (0, 0, k)),
                pl.BlockSpec(coarse.shape, lambda k, s: (0, 0, 0)),
                pl.BlockSpec(fine.shape, lambda k, s: (0, 0, 0)),
            ],
            out_specs=[
                pl.BlockSpec((2, rows, dirs), lambda k, s: (0, 0, 0)),
                pl.BlockSpec((1, dirs), lambda k, s: (0, 0)),
            ],
            scratch_shapes=[
                pltpu.VMEM((2 * rows, dirs), f32),
                pltpu.VMEM((2 * width, dirs), bf16),
                pltpu.VMEM((2 * width, dirs), bf16),
            ],
        ),
        out_shape=[jax.ShapeDtypeStruct((2, rows, dirs), f32), jax.ShapeDtypeStruct((1, dirs), f32)],
        name="steer",
    )(first, inverse, coarse, fine)


def stream(step, count, refs, buf, sem):
    def copy(g, slot):
        return pltpu.make_async_copy(refs[g], buf.at[slot], sem.at[slot])

    @pl.when(step == 0)
    def _():
        copy(0, 0).start()

    for g in range(1, count):

        @pl.when(step + 1 == g)
        def _(g=g):
            copy(g, g % 2).start()

    slot = step % 2
    copy(0, slot).wait()
    return slot


def snap_kernel(count, has_acc, _, p_ref, *refs):
    u_refs = refs[:count]
    out_ref, buf, sem = refs[-3:]
    step = pl.program_id(0)
    slot = stream(step, count, u_refs, buf, sem)
    re_high, re_low = split(p_ref[0])
    im_high, im_low = split(p_ref[1])
    snaps = buf[slot]
    part = mm(embed(re_high, im_high), snaps) + mm(embed(re_low, im_low), snaps)

    @pl.when(step == 0)
    def _():
        out_ref[...] = part + refs[count][...] if has_acc else part

    @pl.when(step > 0)
    def _():
        out_ref[...] += part


def snap_product(inverse, snaps, sources, acc):
    _, rows, _ = inverse.shape
    height, width = snaps[0].shape
    count = len(snaps)
    whole = lambda *_: (0, 0)
    specs = [pl.BlockSpec((2, rows, rows), lambda i, s: (0, 0, s[i]))]
    specs += [pl.BlockSpec(memory_space=pl.ANY)] * count
    args = [inverse] + snaps
    if acc is not None:
        specs.append(pl.BlockSpec((2 * rows, width), whole))
        args.append(acc)
    return pl.pallas_call(
        lambda *refs: snap_kernel(count, acc is not None, *refs),
        grid_spec=pltpu.PrefetchScalarGridSpec(
            num_scalar_prefetch=1,
            grid=(count,),
            in_specs=specs,
            out_specs=pl.BlockSpec((2 * rows, width), whole),
            scratch_shapes=[pltpu.VMEM((2, height, width), bf16), pltpu.SemaphoreType.DMA((2,))],
        ),
        out_shape=jax.ShapeDtypeStruct((2 * rows, width), f32),
        name="snaps",
    )(sources, *args)


def panels(width):
    offsets, at = [], 0
    for start in range(0, width, LANES):
        offsets.append(at)
        at += width - start
    return offsets, at


def cross_kernel(count, has_acc, src_ref, coarse_ref, fine_ref, *refs):
    u_refs, q_refs = refs[:count], refs[count : 2 * count]
    k_ref, b_ref, u_buf, q_buf, a_high, a_low, u_sem, q_sem = refs[-8:]
    step = pl.program_id(0)
    u_slot = stream(step, count, u_refs, u_buf, u_sem)
    q_slot = stream(step, count, q_refs, q_buf, q_sem)
    rows, width = u_buf.shape[1] // 2, u_buf.shape[2]
    inner, dirs = fine_ref.shape[1], fine_ref.shape[2]
    for a in range(rows // inner):
        ar, ai = steer_rows(coarse_ref, fine_ref, src_ref[step] * (rows // inner) + a)
        top, low = slice(a * inner, (a + 1) * inner), slice(rows + a * inner, rows + (a + 1) * inner)
        re, im = split(ar), split(ai)
        for ref, r, i in ((a_high, re[0], im[0]), (a_low, re[1], im[1])):
            ref[top, :dirs], ref[low, :dirs] = r, i
            ref[top, dirs:], ref[low, dirs:] = i, -r

    @pl.when(step == 0)
    def _():
        if has_acc:
            k_ref[...] = refs[2 * count][...]
            b_ref[...] = refs[2 * count + 1][...]
        else:
            k_ref[...] = jnp.zeros(k_ref.shape, f32)
            b_ref[...] = jnp.zeros(b_ref.shape, f32)

    q_high, q_low = split(q_buf[q_slot])
    first_high, first_low = q_high[:, : width // 2], q_low[:, : width // 2]
    b_ref[...] += mm_tn(first_high, a_high[...]) + mm_tn(first_low, a_high[...]) + mm_tn(first_high, a_low[...])
    snaps = u_buf[u_slot]
    offsets, _ = panels(width)
    for start, at in zip(range(0, width, LANES), offsets):
        place = slice(start, start + LANES)
        left = snaps[:, start:]
        part = None
        for q in (q_high, q_low):
            re, im = q[:rows, place], q[rows:, place]
            right = jnp.concatenate([jnp.concatenate([re, im], 1), jnp.concatenate([im, -re], 1)], 0)
            piece = mm_tn(left, right)
            part = piece if part is None else part + piece
        k_ref[at : at + width - start, :] += part


def cross_products(snaps, products, sources, coarse, fine, acc):
    height, width = snaps[0].shape
    count = len(snaps)
    dirs = coarse.shape[2]
    whole = lambda *_: (0, 0)
    shapes = [(panels(width)[1], 2 * LANES), (width // 2, 2 * dirs)]
    specs = [pl.BlockSpec(coarse.shape, lambda *_: (0, 0, 0)), pl.BlockSpec(fine.shape, lambda *_: (0, 0, 0))]
    specs += [pl.BlockSpec(memory_space=pl.ANY)] * (2 * count)
    args = [coarse, fine] + snaps + products
    if acc is not None:
        specs += [pl.BlockSpec(s, whole) for s in shapes]
        args += list(acc)
    return pl.pallas_call(
        lambda *refs: cross_kernel(count, acc is not None, *refs),
        grid_spec=pltpu.PrefetchScalarGridSpec(
            num_scalar_prefetch=1,
            grid=(count,),
            in_specs=specs,
            out_specs=[pl.BlockSpec(s, whole) for s in shapes],
            scratch_shapes=[
                pltpu.VMEM((2, height, width), bf16),
                pltpu.VMEM((2, height, width), f32),
                pltpu.VMEM((height, 2 * dirs), bf16),
                pltpu.VMEM((height, 2 * dirs), bf16),
                pltpu.SemaphoreType.DMA((2,)),
                pltpu.SemaphoreType.DMA((2,)),
            ],
        ),
        out_shape=[jax.ShapeDtypeStruct(s, f32) for s in shapes],
        name="cross",
    )(sources, *args)


def eye(n):
    return (lax.broadcasted_iota(jnp.int32, (n, n), 0) == lax.broadcasted_iota(jnp.int32, (n, n), 1)).astype(f32)


def spd_inverse(matrix, x_ref, r_ref):
    n = matrix.shape[0]
    ident = eye(n)
    norm = jnp.max(jnp.sum(jnp.abs(matrix), axis=0, keepdims=True))
    begin = 1.9 / norm
    coarse = matrix.astype(bf16)
    x_ref[...] = ident * begin

    def rough_residual():
        r = ident - mm(coarse, x_ref[...].astype(bf16))
        r_ref[...] = r
        return jnp.sum(r * r)

    def rough(state):
        size, _, count = state
        x = x_ref[...]
        x_ref[...] = x + mm(x.astype(bf16), r_ref[...].astype(bf16))
        return rough_residual(), size, count + 1

    def rough_more(state):
        size, last, count = state
        return jnp.logical_and(size > 0.05, jnp.logical_and(size < last, count < 32))

    size = rough_residual()
    size, _, _ = lax.while_loop(rough_more, rough, (size, 2.0 * size + 1.0, 0))

    @pl.when(jnp.logical_not(size < 0.25))
    def _():
        x_ref[...] = ident * begin

    def residual():
        r = ident - exact(matrix, x_ref[...])
        r_ref[...] = r
        return jnp.sum(r * r)

    def fine(state):
        size, _, count = state
        x = x_ref[...]
        x_ref[...] = x + exact(x, r_ref[...])
        return residual(), size, count + 1

    def fine_more(state):
        size, last, count = state
        moving = jnp.logical_or(size > 0.25, size < 0.5 * last)
        return jnp.logical_and(size > 1e-5, jnp.logical_and(moving, count < 64))

    size = residual()
    lax.while_loop(fine_more, fine, (size, 4.0 * size, 0))
    x = x_ref[...]
    x = x + exact(x, r_ref[...])
    return 0.5 * (x + x.T)


def quasi_inverse(block, x_ref, r_ref):
    a, c, b = block(0, 0), block(1, 0), block(1, 1)
    first = spd_inverse(0.5 * (a + a.T), x_ref, r_ref)
    v = exact(first, c, ((1,), (1,)))
    schur = exact(c, v) - b
    second = spd_inverse(0.5 * (schur + schur.T), x_ref, r_ref)
    cross = exact(v, second)
    corner = first - exact(cross, v, ((1,), (1,)))
    n = LANES
    re = jnp.concatenate(
        [
            jnp.concatenate([corner[:n, :n], cross[:n, :n]], 1),
            jnp.concatenate([cross[:n, :n].T, -second[:n, :n]], 1),
        ],
        0,
    )
    im = jnp.concatenate(
        [
            jnp.concatenate([corner[n:, :n], cross[n:, :n]], 1),
            jnp.concatenate([-cross[n:, :n].T, -second[n:, :n]], 1),
        ],
        0,
    )
    return re, im


def solve_kernel(window, k_ref, b_ref, q_ref, h_ref, x_ref, h_out, power_ref, s_re, s_im, newton, rest):
    rows, width = q_ref.shape[0] // 2, q_ref.shape[1]
    half = width // 2
    offsets, _ = panels(width)

    def tile(p, q):
        at = offsets[q] + (p - q) * LANES
        m = k_ref[at : at + LANES, :]
        return m[:, :LANES], m[:, LANES:]

    def diagonal(p):
        return (window if p % 2 == 0 else -window) * eye(2 * LANES)

    def first_block(p, q):
        e = embed(*tile(p, q))
        return e + diagonal(p) if p == q else e

    g_re, g_im = quasi_inverse(first_block, newton, rest)
    k21 = [[tile(p, q) for q in (0, 1)] for p in (2, 3)]
    k21_re = jnp.concatenate([jnp.concatenate([t[0] for t in line], 1) for line in k21], 0)
    k21_im = jnp.concatenate([jnp.concatenate([t[1] for t in line], 1) for line in k21], 0)
    g_emb = embed(g_re, g_im)
    w = exact(g_emb, jnp.concatenate([k21_re.T, -k21_im.T], 0))
    w_re, w_im = w[:half], w[half:]
    fold = exact(embed(k21_re, k21_im), w)
    s_re[...], s_im[...] = fold[:half], fold[half:]

    def second_block(p, q):
        at, to = slice(p * LANES, (p + 1) * LANES), slice(q * LANES, (q + 1) * LANES)
        re, im = tile(p + 2, q + 2)
        e = embed(re - s_re[at, to], im - s_im[at, to])
        return e + diagonal(p) if p == q else e

    i_re, i_im = quasi_inverse(second_block, newton, rest)
    q1 = jnp.concatenate([q_ref[:rows, :half], q_ref[rows:, :half]], 1)
    q2 = jnp.concatenate([q_ref[:rows, half:], q_ref[rows:, half:]], 1)
    y = exact(q1, embed(g_re, -g_im))
    x2 = exact(q2 - exact(q1, embed(w_re, -w_im)), embed(i_re, -i_im))
    x1 = y - exact(x2, embed(w_re.T, w_im.T))
    x_ref[:, :half], x_ref[:, half:width] = x1[:, :half], x2[:, :half]
    x_ref[:, width : width + half], x_ref[:, width + half :] = x1[:, half:], x2[:, half:]
    dirs = h_ref.shape[2]
    b = jnp.concatenate([b_ref[:, :dirs], b_ref[:, dirs:]], 0)
    gb = exact(g_emb, b)
    power_ref[...] = jnp.sum(b * gb, axis=0, keepdims=True)
    h = exact(embed(q_ref[:rows, :half], q_ref[rows:, :half]), gb)
    h_out[0] = h_ref[0] - h[:rows]
    h_out[1] = h_ref[1] - h[rows:]


def solve(window, kmat, bmat, local, h):
    width = local.shape[1]
    rows, dirs = h.shape[1], h.shape[2]
    return pl.pallas_call(
        lambda *refs: solve_kernel(window, *refs),
        out_shape=[
            jax.ShapeDtypeStruct((rows, 2 * width), f32),
            jax.ShapeDtypeStruct(h.shape, f32),
            jax.ShapeDtypeStruct((1, dirs), f32),
        ],
        scratch_shapes=[pltpu.VMEM((width // 2, width // 2), f32)] * 2 + [pltpu.VMEM((2 * LANES, 2 * LANES), f32)] * 2,
        name="solve",
    )(kmat, bmat, local, h)


def update_kernel(count, _, p_ref, x_ref, *refs):
    q_refs = refs[:count]
    out_ref, buf, x_high, x_low, sem = refs[count:]
    step = pl.program_id(0)
    rows = p_ref.shape[1]
    width = x_ref.shape[1] // 2

    @pl.when(step == 0)
    def _():
        high, low = split(x_ref[...])
        for ref, v in ((x_high, high), (x_low, low)):
            ref[:rows, :] = v
            ref[rows:, :width], ref[rows:, width:] = v[:, width:], -v[:, :width]

    slot = stream(step, count, q_refs, buf, sem)
    q_high, q_low = split(jnp.concatenate([buf[slot, :rows, :], buf[slot, rows:, :]], 1))
    part = mm_nt(x_high[...], q_high) + mm_nt(x_low[...], q_high) + mm_nt(x_high[...], q_low)
    out_ref[0] = p_ref[0] - part[:rows]
    out_ref[1] = p_ref[1] - part[rows:]


def update(inverse, x, products, sources):
    _, rows, length = inverse.shape
    width = x.shape[1] // 2
    count = len(products)
    return pl.pallas_call(
        lambda *refs: update_kernel(count, *refs),
        grid_spec=pltpu.PrefetchScalarGridSpec(
            num_scalar_prefetch=1,
            grid=(count,),
            in_specs=[
                pl.BlockSpec((2, rows, rows), lambda i, s: (0, 0, s[i])),
                pl.BlockSpec((rows, 2 * width), lambda i, s: (0, 0)),
            ]
            + [pl.BlockSpec(memory_space=pl.ANY)] * count,
            out_specs=pl.BlockSpec((2, rows, rows), lambda i, s: (0, 0, s[i])),
            scratch_shapes=[
                pltpu.VMEM((2, 2 * rows, width), f32),
                pltpu.VMEM((2 * rows, 2 * width), bf16),
                pltpu.VMEM((2 * rows, 2 * width), bf16),
                pltpu.SemaphoreType.DMA((2,)),
            ],
        ),
        out_shape=jax.ShapeDtypeStruct(inverse.shape, f32),
        name="update",
    )(sources, inverse, x, *products)


def on_device(row_count, inverse, cycle, arrivals, departing, directions):
    rows, length = inverse.shape[1], inverse.shape[2]
    window = cycle.shape[2]
    snap = arrivals.shape[3]
    dirs = directions.shape[1]
    inner = 64
    first = (lax.axis_index("row") * (rows // inner)).astype(jnp.int32)[None]
    sources = ring_sources(row_count)
    right_count, left_count = ring_counts(row_count)

    slots = departing.reshape(-1)
    pick = (jnp.arange(window, dtype=jnp.int32)[:, None] == slots[None, :]).astype(bf16)
    departed = mm(cycle.reshape(2 * rows, window), pick).astype(bf16)
    blocks = []
    for t in range(STEPS):
        blocks += [arrivals[t].reshape(2 * rows, snap), departed[:, t * snap : (t + 1) * snap]]
    own = jnp.concatenate(blocks, 1)

    tables = [steering_tables(directions[t], length, inner) for t in range(STEPS)]
    part = dirs // 2
    pieces = [
        (coarse[:, :, s : s + part], fine[:, :, s : s + part]) for coarse, fine in tables for s in range(0, dirs, part)
    ]
    done = []

    def steer(after):
        after, place = together(after, first)
        done.append(steer_product(inverse, *pieces[len(done)], place))
        return after

    mine = [[own]]
    theirs = [[swap(own, row_count)]]
    right = left = own
    acc, folded = None, 0
    for h in range(1, right_count + 1):
        held = (right, left)
        moved_right = hop(right, row_count, 1)
        moved_left = hop(left, row_count, -1) if h <= left_count else left
        if len(done) < len(pieces) - 1:
            steer(held)
        if h % 2 == 0 or len(done) >= len(pieces) - 1:
            ready = range(folded, h)
            snaps = [u for g in ready for u in mine[g] + theirs[g]]
            where = jnp.concatenate([s for g in ready for s in sources[g]])
            acc = snap_product(inverse, snaps, where, acc)
            folded = h
        (right, left, last, acc) = together(moved_right, moved_left, done[-1], acc)
        done[-1] = last
        group = [right, left] if h <= left_count else [right]
        mine.append(group)
        theirs.append([swap(u, row_count) for u in group])
    ready = range(folded, right_count + 1)
    snaps = [u for g in ready for u in mine[g] + theirs[g]]
    local = snap_product(inverse, snaps, jnp.concatenate([s for g in ready for s in sources[g]]), acc)

    sent = lax.optimization_barrier(local.astype(jnp.float16))
    right = left = sent
    wide = [[sent.astype(f32)]]
    coarse, fine = tables[1]
    acc, folded = None, 0
    for h in range(1, right_count + 1):
        held = (right, left)
        moved_right = hop(right, row_count, 1)
        moved_left = hop(left, row_count, -1) if h <= left_count else left
        if len(done) < len(pieces):
            steer(held)
        if h > 1:
            ready = range(folded, h)
            acc = cross_products(
                [u for g in ready for u in mine[g]],
                [q for g in ready for q in wide[g]],
                jnp.concatenate([sources[g][0] for g in ready]),
                coarse,
                fine,
                acc,
            )
            folded = h
        (right, left, last, acc) = together(moved_right, moved_left, done[-1], acc)
        done[-1] = last
        wide.append([q.astype(f32) for q in ([right, left] if h <= left_count else [right])])
    ready = range(folded, right_count + 1)
    kmat, bmat = cross_products(
        [u for g in ready for u in mine[g]],
        [q for g in ready for q in wide[g]],
        jnp.concatenate([sources[g][0] for g in ready]),
        coarse,
        fine,
        acc,
    )
    kmat = kmat + swap(kmat, row_count)
    bmat = bmat + swap(bmat, row_count)
    wide_mine = [q for group in wide for q in group]
    wide_theirs = [swap(q, row_count) for q in wide_mine]

    steered = [
        jnp.concatenate([done[i][0] for i in range(len(pieces)) if i * part // dirs == t], 2) for t in range(STEPS)
    ]
    power = tree_sum(jnp.concatenate([p for _, p in done], 0), row_count).reshape(STEPS, dirs)
    x, second, fold = solve(float(window), kmat, bmat, local, steered[1])
    power = jnp.concatenate([power[:1], power[1:] - fold], 0)
    where = jnp.concatenate([m for m, _ in sources] + [t for _, t in sources])
    new_inverse = update(inverse, x, wide_mine + wide_theirs, where)
    spectrum = length / power
    weights = jnp.stack([steered[0] * spectrum[0], second * spectrum[1]])
    return new_inverse, weights, spectrum


def solution(mesh):
    row_count = mesh.shape["row"]
    in_specs = (
        P("groups", "row", None),
        P("groups", "row", None),
        P("groups", None, "row", None),
        P("groups", None),
        P("groups", None),
    )
    out_specs = (P("groups", "row", None), P("groups", None, "row", None), P("groups", None))
    return jax.shard_map(
        lambda *args: on_device(row_count, *args), mesh=mesh, in_specs=in_specs, out_specs=out_specs, check_vma=False
    )
```

```python
import jax
import jax.numpy as jnp
from jax import lax
from jax.experimental import pallas as pl
from jax.experimental.pallas import tpu as pltpu
from jax.sharding import PartitionSpec as P

STEPS = 2

f32 = jnp.float32
bf16 = jnp.bfloat16
HIGHEST = lax.Precision.HIGHEST
LANES = 128


def split(x):
    high = x.astype(bf16)
    return high, (x - high.astype(f32)).astype(bf16)


def mm(left, right):
    return jnp.dot(left, right, preferred_element_type=f32)


def mm_tn(left, right):
    return lax.dot_general(left, right, (((0,), (0,)), ((), ())), preferred_element_type=f32)


def mm_nt(left, right):
    return lax.dot_general(left, right, (((1,), (1,)), ((), ())), preferred_element_type=f32)


def exact(left, right, dims=((1,), (0,))):
    return lax.dot_general(left, right, (dims, ((), ())), precision=HIGHEST, preferred_element_type=f32)


def ring_order(row_count):
    chips = row_count // 2
    return list(range(0, chips, 2)) + list(reversed(range(1, chips, 2)))


def hop(block, row_count, shift):
    order = ring_order(row_count)
    chips = len(order)
    pairs = [(order[i] * 2 + core, order[(i + shift) % chips] * 2 + core) for i in range(chips) for core in range(2)]
    return lax.ppermute(block, "row", pairs)


def swap(block, row_count):
    return lax.ppermute(block, "row", [(i, i ^ 1) for i in range(row_count)])


def ring_counts(row_count):
    chips = row_count // 2
    right = chips // 2
    return right, chips - 1 - right


def together(*trees):
    return lax.optimization_barrier(trees)


def ring_chips(row_count):
    order = ring_order(row_count)
    chips = len(order)
    position = [0] * chips
    for place, chip in enumerate(order):
        position[chip] = place
    here = jnp.asarray(position, jnp.int32)[lax.axis_index("row") // 2]
    right, left = ring_counts(row_count)
    shifts, ends = [0], [1]
    for h in range(1, right + 1):
        shifts += [-h, h] if h <= left else [-h]
        ends.append(len(shifts))
    return jnp.asarray(order, jnp.int32)[(here + jnp.asarray(shifts, jnp.int32)) % chips], ends


def exchange(x, stride, row_count):
    if stride >= row_count or row_count & (row_count - 1):
        return jnp.zeros_like(x)
    return lax.ppermute(x, "row", [(i, i ^ stride) for i in range(row_count)])


def steering_tables(directions, length, inner):
    odd = 2 * directions[None, :] + 1 - 2 * length
    halves = jnp.concatenate(
        [
            jnp.arange(length // inner, dtype=jnp.int32) * (2 * inner),
            jnp.arange(inner, dtype=jnp.int32) * 2,
            jnp.arange(inner, dtype=jnp.int32) * 2 + 1,
            jnp.full((8,), length - 1, jnp.int32),
        ]
    )
    turns = (halves[:, None] * odd) % (8 * length)
    phase = jnp.pi * turns.astype(f32) / (4 * length)
    table = jnp.stack([jnp.cos(phase), jnp.sin(phase)])
    at = length // inner
    return table[:, :at], table[:, at : at + inner], table[:, at + inner : at + 2 * inner], table[:, at + 2 * inner :]


def steer_rows(coarse_ref, fine_ref, index):
    er, ei = coarse_ref[0, pl.ds(index, 1), :], coarse_ref[1, pl.ds(index, 1), :]
    fr, fi = fine_ref[0], fine_ref[1]
    return er * fr - ei * fi, er * fi + ei * fr


def embed(re, im):
    return jnp.concatenate([jnp.concatenate([re, -im], 1), jnp.concatenate([im, re], 1)], 0)


def steer_kernel(first_ref, right_ref, left_ref, coarse_ref, fine_ref, shifted_ref, centre_ref, h_ref, power_ref, *scratch):
    step = pl.program_id(0)
    rows, width = right_ref.shape[1], right_ref.shape[2]
    inner, dirs = fine_ref.shape[1], fine_ref.shape[2]
    a_high, a_low, flip = scratch
    count = width // inner
    side = flip.shape[0]

    @pl.when(step == 0)
    def _():
        row = lax.broadcasted_iota(jnp.int32, (side, side), 0)
        flip[...] = (row + lax.broadcasted_iota(jnp.int32, (side, side), 1) == side - 1).astype(f32).astype(bf16)

    for a in range(count):
        ar, ai = steer_rows(coarse_ref, shifted_ref, step * count + a)
        top, low = slice(a * inner, (a + 1) * inner), slice(width + a * inner, width + (a + 1) * inner)
        a_high[top, :], a_low[top, :] = split(ar)
        a_high[low, :], a_low[low, :] = split(ai)
    left = left_ref[...].reshape(2 * rows, width)
    stack = jnp.concatenate(split(left), 0)
    pieces = []
    for start in range(width - side, -1, -side):
        turned = mm(stack[:, start : start + side], flip[...])
        pieces.append(turned[: 2 * rows] + turned[2 * rows :])
    left = jnp.concatenate(pieces, 1)
    right = right_ref[...].reshape(2 * rows, width)
    even_high, even_low = split(right + left)
    odd_high, odd_low = split(right - left)

    def combined(even, odd):
        turned = jnp.concatenate([-odd[rows:], odd[:rows]], 0)
        return jnp.concatenate([even, turned], 1)

    high = combined(even_high, odd_high)
    part = mm(high, a_high[...]) + mm(combined(even_low, odd_low), a_high[...]) + mm(high, a_low[...])

    @pl.when(step == 0)
    def _():
        h_ref[...] = part

    @pl.when(step > 0)
    def _():
        h_ref[...] += part

    @pl.when(step == pl.num_programs(0) - 1)
    def _():
        re, im = h_ref[:rows, :], h_ref[rows:, :]
        cr, ci = centre_ref[0, :1, :], centre_ref[1, :1, :]
        h_ref[:rows, :] = re * cr - im * ci
        h_ref[rows:, :] = re * ci + im * cr
        power = jnp.zeros((1, dirs), f32)
        for a in range(rows // inner):
            ar, ai = steer_rows(coarse_ref, fine_ref, first_ref[0] + a)
            top, low = slice(a * inner, (a + 1) * inner), slice(rows + a * inner, rows + (a + 1) * inner)
            power += jnp.sum(ar * h_ref[top, :] + ai * h_ref[low, :], axis=0, keepdims=True)
        power_ref[...] = power


def steer_product(inverse, tables, first):
    _, rows, length = inverse.shape
    dirs = tables[0].shape[2]
    width = min(512, length // 2)
    steps = length // 2 // width
    side = min(2 * LANES, width)
    whole = lambda k, s: (0, 0)
    return pl.pallas_call(
        steer_kernel,
        grid_spec=pltpu.PrefetchScalarGridSpec(
            num_scalar_prefetch=1,
            grid=(steps,),
            in_specs=[
                pl.BlockSpec((2, rows, width), lambda k, s: (0, 0, steps + k)),
                pl.BlockSpec((2, rows, width), lambda k, s: (0, 0, steps - 1 - k)),
            ]
            + [pl.BlockSpec(t.shape, lambda k, s: (0, 0, 0)) for t in tables],
            out_specs=[pl.BlockSpec((2 * rows, dirs), whole), pl.BlockSpec((1, dirs), whole)],
            scratch_shapes=[
                pltpu.VMEM((2 * width, dirs), bf16),
                pltpu.VMEM((2 * width, dirs), bf16),
                pltpu.VMEM((side, side), bf16),
            ],
        ),
        out_shape=[jax.ShapeDtypeStruct((2 * rows, dirs), f32), jax.ShapeDtypeStruct((1, dirs), f32)],
        name="steer",
    )(first, inverse, inverse, *tables)


def whole_block(array):
    return ((array, 0), (array, array.shape[0] // 2))


def arrays_of(blocks):
    arrays, places = [], {}
    for block in blocks:
        for array, _ in block:
            if id(array) not in places:
                places[id(array)] = len(arrays)
                arrays.append(array)
    return arrays, [tuple((places[id(array)], row) for array, row in block) for block in blocks]


def stream(step, plan, refs, buf, sem, where):
    def copies(g, slot):
        out = []
        for k, block in enumerate(plan[g]):
            for plane, (array, row) in enumerate(block):
                start, rows = where(k, plane)
                source = refs[array].at[pl.ds(row, rows), :]
                out.append(pltpu.make_async_copy(source, buf.at[slot, pl.ds(start, rows), :], sem.at[slot]))
        return out

    @pl.when(step == 0)
    def _():
        for c in copies(0, 0):
            c.start()

    for g in range(1, len(plan)):

        @pl.when(step + 1 == g)
        def _(g=g):
            for c in copies(g, g % 2):
                c.start()

    slot = step % 2
    pltpu.make_async_copy(buf.at[slot], buf.at[slot], sem.at[slot]).wait()
    return slot


def snap_kernel(plan, has_acc, chip_ref, core_ref, p_ref, *refs):
    out_ref, buf, sem = refs[-3:]
    step = pl.program_id(0)
    rows = p_ref.shape[1]
    core = core_ref[0]

    def where(k, plane):
        return pl.multiple_of((2 * plane + (core if k == 0 else 1 - core)) * rows, rows), rows

    slot = stream(step, plan, refs, buf, sem, where)
    re_high, re_low = split(p_ref[0])
    im_high, im_low = split(p_ref[1])
    snaps = buf[slot]
    part = mm(embed(re_high, im_high), snaps) + mm(embed(re_low, im_low), snaps)

    @pl.when(step == 0)
    def _():
        out_ref[...] = part + refs[-4][...] if has_acc else part

    @pl.when(step > 0)
    def _():
        out_ref[...] += part


def snap_product(inverse, mine, theirs, chips, begin, core, acc):
    _, rows, _ = inverse.shape
    arrays, plan = arrays_of(mine + theirs)
    count = len(mine)
    plan = [[plan[g], plan[count + g]] for g in range(count)]
    width = arrays[0].shape[1]
    whole = lambda *_: (0, 0)
    specs = [pl.BlockSpec((2, rows, 2 * rows), lambda i, s, c: (0, 0, s[begin + i]))]
    specs += [pl.BlockSpec(memory_space=pltpu.HBM)] * len(arrays)
    args = [inverse] + arrays
    if acc is not None:
        specs.append(pl.BlockSpec((2 * rows, width), whole))
        args.append(acc)
    return pl.pallas_call(
        lambda *refs: snap_kernel(plan, acc is not None, *refs),
        grid_spec=pltpu.PrefetchScalarGridSpec(
            num_scalar_prefetch=2,
            grid=(count,),
            in_specs=specs,
            out_specs=pl.BlockSpec((2 * rows, width), whole),
            scratch_shapes=[pltpu.VMEM((2, 4 * rows, width), bf16), pltpu.SemaphoreType.DMA((2,))],
        ),
        out_shape=jax.ShapeDtypeStruct((2 * rows, width), f32),
        name="snaps",
    )(chips, core, *args)


def panels(width):
    offsets, at = [], 0
    for start in range(0, width, 2 * LANES):
        offsets.append(at)
        at += width - start
    return offsets, at


def cross_kernel(u_plan, q_plan, u_count, q_count, has_acc, begin, chip_ref, core_ref, coarse_ref, fine_ref, *refs):
    u_refs, q_refs = refs[:u_count], refs[u_count : u_count + q_count]
    k_ref, b_ref, u_buf, q_buf, a_high, a_low, u_sem, q_sem = refs[-8:]
    step = pl.program_id(0)
    rows, width = u_buf.shape[1] // 2, u_buf.shape[2]

    def where(k, plane):
        return plane * rows, rows

    u_slot = stream(step, u_plan, u_refs, u_buf, u_sem, where)
    q_slot = stream(step, q_plan, q_refs, q_buf, q_sem, where)
    inner, dirs = fine_ref.shape[1], fine_ref.shape[2]
    source = chip_ref[begin + step] * 2 + core_ref[0]
    for a in range(rows // inner):
        ar, ai = steer_rows(coarse_ref, fine_ref, source * (rows // inner) + a)
        top, low = slice(a * inner, (a + 1) * inner), slice(rows + a * inner, rows + (a + 1) * inner)
        re, im = split(ar), split(ai)
        for ref, r, i in ((a_high, re[0], im[0]), (a_low, re[1], im[1])):
            ref[top, :dirs], ref[low, :dirs] = r, i
            ref[top, dirs:], ref[low, dirs:] = i, -r

    q_high, q_low = split(q_buf[q_slot])
    first_high, first_low = q_high[:, : width // 2], q_low[:, : width // 2]
    b_part = mm_tn(first_high, a_high[...]) + mm_tn(first_low, a_high[...]) + mm_tn(first_high, a_low[...])
    snaps = u_buf[u_slot]
    parts = []
    for start in range(0, width, 2 * LANES):
        left = snaps[:, start:]
        part = None
        for q in (q_high, q_low):
            re, im = q[:rows, start : start + 2 * LANES], q[rows:, start : start + 2 * LANES]
            piece = mm_tn(left, jnp.concatenate([jnp.concatenate([re, im], 1), jnp.concatenate([im, -re], 1)], 0))
            part = piece if part is None else part + piece
        parts.append(part)
    offsets, total = panels(width)
    ends = offsets[1:] + [total]

    @pl.when(step == 0)
    def _():
        b_ref[...] = b_part + refs[-9][...] if has_acc else b_part
        for at, end, part in zip(offsets, ends, parts):
            k_ref[at:end, :] = part + refs[-10][at:end, :] if has_acc else part

    @pl.when(step > 0)
    def _():
        b_ref[...] += b_part
        for at, end, part in zip(offsets, ends, parts):
            k_ref[at:end, :] += part


def cross_products(snaps, products, chips, begin, core, coarse, fine, acc):
    u_arrays, u_plan = arrays_of(snaps)
    q_arrays, q_plan = arrays_of(products)
    u_plan, q_plan = [[u] for u in u_plan], [[q] for q in q_plan]
    width = u_arrays[0].shape[1]
    height = coarse.shape[1] * fine.shape[1] * 2 // (chips.shape[0] * 2)
    count = len(snaps)
    dirs = coarse.shape[2]
    whole = lambda *_: (0, 0)
    shapes = [(panels(width)[1], 4 * LANES), (width // 2, 2 * dirs)]
    specs = [pl.BlockSpec(coarse.shape, lambda *_: (0, 0, 0)), pl.BlockSpec(fine.shape, lambda *_: (0, 0, 0))]
    specs += [pl.BlockSpec(memory_space=pltpu.HBM)] * len(u_arrays) + [pl.BlockSpec(memory_space=pl.ANY)] * len(q_arrays)
    args = [coarse, fine] + u_arrays + q_arrays
    if acc is not None:
        specs += [pl.BlockSpec(s, whole) for s in shapes]
        args += list(acc)
    return pl.pallas_call(
        lambda *refs: cross_kernel(u_plan, q_plan, len(u_arrays), len(q_arrays), acc is not None, begin, *refs),
        grid_spec=pltpu.PrefetchScalarGridSpec(
            num_scalar_prefetch=2,
            grid=(count,),
            in_specs=specs,
            out_specs=[pl.BlockSpec(s, whole) for s in shapes],
            scratch_shapes=[
                pltpu.VMEM((2, height, width), bf16),
                pltpu.VMEM((2, height, width), f32),
                pltpu.VMEM((height, 2 * dirs), bf16),
                pltpu.VMEM((height, 2 * dirs), bf16),
                pltpu.SemaphoreType.DMA((2,)),
                pltpu.SemaphoreType.DMA((2,)),
            ],
        ),
        out_shape=[jax.ShapeDtypeStruct(s, f32) for s in shapes],
        name="cross",
    )(chips, core, *args)


def near(left, right, dims=((1,), (0,))):
    left_high, left_low = split(left)
    right_high, right_low = split(right)
    dot = lambda a, b: lax.dot_general(a, b, (dims, ((), ())), preferred_element_type=f32)
    return dot(left_high, right_high) + dot(left_low, right_high) + dot(left_high, right_low)


def eye(n):
    return (lax.broadcasted_iota(jnp.int32, (n, n), 0) == lax.broadcasted_iota(jnp.int32, (n, n), 1)).astype(f32)


def spd_inverse(matrix, x_ref, r_ref):
    n = matrix.shape[0]
    ident = eye(n)
    norm = jnp.max(jnp.sum(jnp.abs(matrix), axis=0, keepdims=True))
    begin = 1.9 / norm
    coarse = matrix.astype(bf16)
    x_ref[...] = ident * begin

    def rough_residual():
        r = ident - mm(coarse, x_ref[...].astype(bf16))
        r_ref[...] = r
        return jnp.sum(r * r)

    def rough(state):
        size, _, count = state
        x = x_ref[...]
        x_ref[...] = x + mm(x.astype(bf16), r_ref[...].astype(bf16))
        return rough_residual(), size, count + 1

    def rough_more(state):
        size, last, count = state
        return jnp.logical_and(size > 0.05, jnp.logical_and(size < last, count < 32))

    size = rough_residual()
    size, _, _ = lax.while_loop(rough_more, rough, (size, 2.0 * size + 1.0, 0))

    @pl.when(jnp.logical_not(size < 0.25))
    def _():
        x_ref[...] = ident * begin

    def residual():
        r = ident - exact(matrix, x_ref[...])
        r_ref[...] = r
        return jnp.sum(r * r)

    def fine(state):
        size, _, count = state
        x = x_ref[...]
        x_ref[...] = x + near(x, r_ref[...])
        return residual(), size, count + 1

    def fine_more(state):
        size, last, count = state
        moving = jnp.logical_or(size > 0.25, size < 0.5 * last)
        return jnp.logical_and(size > 1e-5, jnp.logical_and(moving, count < 64))

    size = residual()
    lax.while_loop(fine_more, fine, (size, 4.0 * size, 0))
    x = x_ref[...]
    x = x + mm(x.astype(bf16), r_ref[...].astype(bf16))
    return 0.5 * (x + x.T)


def quasi_inverse(block, x_ref, r_ref):
    a, c, b = block(0, 0), block(1, 0), block(1, 1)
    first = spd_inverse(0.5 * (a + a.T), x_ref, r_ref)
    v = near(first, c, ((1,), (1,)))
    schur = near(c, v) - b
    second = spd_inverse(0.5 * (schur + schur.T), x_ref, r_ref)
    cross = near(v, second)
    corner = first - near(cross, v, ((1,), (1,)))
    n = LANES
    re = jnp.concatenate(
        [
            jnp.concatenate([corner[:n, :n], cross[:n, :n]], 1),
            jnp.concatenate([cross[:n, :n].T, -second[:n, :n]], 1),
        ],
        0,
    )
    im = jnp.concatenate(
        [
            jnp.concatenate([corner[n:, :n], cross[n:, :n]], 1),
            jnp.concatenate([-cross[n:, :n].T, -second[n:, :n]], 1),
        ],
        0,
    )
    return re, im


def solve_kernel(window, k_ref, k_more, b_any, b_more_any, q_any, h_any, x_ref, h_out, power_ref, *scratch):
    s_re, s_im, newton, rest, b_ref, b_more, q_ref, h_ref, sem = scratch
    pairs = ((q_any, q_ref), (b_any, b_ref), (b_more_any, b_more), (h_any, h_ref))
    late = [pltpu.make_async_copy(source, target, sem.at[i]) for i, (source, target) in enumerate(pairs)]
    for copy in late:
        copy.start()
    rows, width = q_ref.shape[0] // 2, q_ref.shape[1]
    half = width // 2
    offsets, _ = panels(width)

    def tile(p, q):
        at = offsets[q // 2] + (p - q // 2 * 2) * LANES
        m = k_ref[at : at + LANES, :] + k_more[at : at + LANES, :]
        start = (q % 2) * LANES
        return m[:, start : start + LANES], m[:, 2 * LANES + start : 3 * LANES + start]

    def diagonal(p):
        return (window if p % 2 == 0 else -window) * eye(2 * LANES)

    def first_block(p, q):
        e = embed(*tile(p, q))
        return e + diagonal(p) if p == q else e

    g_re, g_im = quasi_inverse(first_block, newton, rest)
    k21 = [[tile(p, q) for q in (0, 1)] for p in (2, 3)]
    k21_re = jnp.concatenate([jnp.concatenate([t[0] for t in line], 1) for line in k21], 0)
    k21_im = jnp.concatenate([jnp.concatenate([t[1] for t in line], 1) for line in k21], 0)
    g_emb = embed(g_re, g_im)
    w = near(g_emb, jnp.concatenate([k21_re.T, -k21_im.T], 0))
    w_re, w_im = w[:half], w[half:]
    fold = near(embed(k21_re, k21_im), w)
    s_re[...], s_im[...] = fold[:half], fold[half:]

    def second_block(p, q):
        at, to = slice(p * LANES, (p + 1) * LANES), slice(q * LANES, (q + 1) * LANES)
        re, im = tile(p + 2, q + 2)
        e = embed(re - s_re[at, to], im - s_im[at, to])
        return e + diagonal(p) if p == q else e

    i_re, i_im = quasi_inverse(second_block, newton, rest)
    for copy in late:
        copy.wait()
    q1 = jnp.concatenate([q_ref[:rows, :half], q_ref[rows:, :half]], 1)
    q2 = jnp.concatenate([q_ref[:rows, half:], q_ref[rows:, half:]], 1)
    y = near(q1, embed(g_re, -g_im))
    x2 = near(q2 - near(q1, embed(w_re, -w_im)), embed(i_re, -i_im))
    x1 = y - near(x2, embed(w_re.T, w_im.T))
    x_ref[:, :half], x_ref[:, half:width] = x1[:, :half], x2[:, :half]
    x_ref[:, width : width + half], x_ref[:, width + half :] = x1[:, half:], x2[:, half:]
    dirs = h_ref.shape[1]
    b = b_ref[...] + b_more[...]
    b = jnp.concatenate([b[:, :dirs], b[:, dirs:]], 0)
    gb = near(g_emb, b)
    power_ref[...] = jnp.sum(b * gb, axis=0, keepdims=True)
    h_out[...] = h_ref[...] - near(embed(q_ref[:rows, :half], q_ref[rows:, :half]), gb)


def solve(window, kmats, bmats, local, h):
    width = local.shape[1]
    rows, dirs = h.shape[0] // 2, h.shape[1]
    return pl.pallas_call(
        lambda *refs: solve_kernel(window, *refs),
        out_shape=[
            jax.ShapeDtypeStruct((rows, 2 * width), f32),
            jax.ShapeDtypeStruct(h.shape, f32),
            jax.ShapeDtypeStruct((1, dirs), f32),
        ],
        in_specs=[pl.BlockSpec(memory_space=pltpu.VMEM)] * 2 + [pl.BlockSpec(memory_space=pl.ANY)] * 4,
        scratch_shapes=[pltpu.VMEM((width // 2, width // 2), f32)] * 2
        + [pltpu.VMEM((2 * LANES, 2 * LANES), f32)] * 2
        + [pltpu.VMEM(a.shape, f32) for a in (*bmats, local, h)]
        + [pltpu.SemaphoreType.DMA((4,))],
        name="solve",
    )(*kmats, *bmats, local, h)


def update_kernel(plan, chip_ref, core_ref, p_ref, x_ref, h0_ref, h1_ref, scale_ref, *refs):
    out_ref, weight_ref, buf, x_high, x_low, sem = refs[-6:]
    step = pl.program_id(0)
    rows = p_ref.shape[1]
    width = x_ref.shape[1] // 2
    core = core_ref[0]

    @pl.when(step == 0)
    def _():
        high, low = split(x_ref[...])
        for ref, v in ((x_high, high), (x_low, low)):
            ref[:rows, :] = v
            ref[rows:, :width], ref[rows:, width:] = v[:, width:], -v[:, :width]

    def where(k, plane):
        return pl.multiple_of((2 * plane + (core if k == 0 else 1 - core)) * rows, rows), rows

    slot = stream(step, plan, refs, buf, sem, where)
    q_high, q_low = split(jnp.concatenate([buf[slot, : 2 * rows, :], buf[slot, 2 * rows :, :]], 1))
    part = mm_nt(x_high[...], q_high) + mm_nt(x_low[...], q_high) + mm_nt(x_high[...], q_low)
    out_ref[0] = p_ref[0] - part[:rows]
    out_ref[1] = p_ref[1] - part[rows:]
    weight_ref[0] = h0_ref[...] * scale_ref[:1, :]
    weight_ref[1] = h1_ref[...] * scale_ref[1:2, :]


def update(inverse, x, mine, theirs, chips, core, steered, scale):
    _, rows, length = inverse.shape
    width = x.shape[1] // 2
    arrays, plan = arrays_of(mine + theirs)
    count = len(mine)
    plan = [[plan[g], plan[count + g]] for g in range(count)]
    dirs = scale.shape[1]
    piece = 2 * rows // count
    return pl.pallas_call(
        lambda *refs: update_kernel(plan, *refs),
        grid_spec=pltpu.PrefetchScalarGridSpec(
            num_scalar_prefetch=2,
            grid=(count,),
            in_specs=[
                pl.BlockSpec((2, rows, 2 * rows), lambda i, s, c: (0, 0, s[i])),
                pl.BlockSpec((rows, 2 * width), lambda i, s, c: (0, 0)),
                pl.BlockSpec((piece, dirs), lambda i, s, c: (i, 0)),
                pl.BlockSpec((piece, dirs), lambda i, s, c: (i, 0)),
                pl.BlockSpec(scale.shape, lambda i, s, c: (0, 0)),
            ]
            + [pl.BlockSpec(memory_space=pl.ANY)] * len(arrays),
            out_specs=[
                pl.BlockSpec((2, rows, 2 * rows), lambda i, s, c: (0, 0, s[i])),
                pl.BlockSpec((2, piece, dirs), lambda i, s, c: (0, i, 0)),
            ],
            scratch_shapes=[
                pltpu.VMEM((2, 4 * rows, width), f32),
                pltpu.VMEM((2 * rows, 2 * width), bf16),
                pltpu.VMEM((2 * rows, 2 * width), bf16),
                pltpu.SemaphoreType.DMA((2,)),
            ],
        ),
        out_shape=[jax.ShapeDtypeStruct(inverse.shape, f32), jax.ShapeDtypeStruct((2, 2 * rows, dirs), f32)],
        name="update",
    )(chips, core, inverse, x, *steered, scale, *arrays)


def on_device(row_count, inverse, cycle, arrivals, departing, directions):
    rows, length = inverse.shape[1], inverse.shape[2]
    window = cycle.shape[2]
    snap = arrivals.shape[3]
    dirs = directions.shape[1]
    inner = 64
    me = lax.axis_index("row").astype(jnp.int32)
    first = (me * (rows // inner))[None]
    core = (me % 2)[None]
    chips, ends = ring_chips(row_count)
    right_count, left_count = ring_counts(row_count)

    slots = departing.reshape(-1)
    pick = (jnp.arange(window, dtype=jnp.int32)[:, None] == slots[None, :]).astype(bf16)
    departed = mm(cycle.reshape(2 * rows, window), pick).astype(bf16)
    blocks = []
    for t in range(STEPS):
        blocks += [arrivals[t].reshape(2 * rows, snap), departed[:, t * snap : (t + 1) * snap]]
    own = jnp.concatenate(blocks, 1)

    tables = [steering_tables(directions[t], length, inner) for t in range(STEPS)]
    steered, powers = [], []

    def steer(after):
        after, place = together(after, first)
        return steer_product(inverse, tables[len(steered)], place)

    def travel(block, work):
        right = left = block
        for h in range(1, right_count + 1):
            held = (right, left)
            moved_right = hop(right, row_count, 1)
            moved_left = hop(left, row_count, -1) if h <= left_count else left
            result = work(h, held)
            right, left, result = together(moved_right, moved_left, result)
            yield h, ([right, left] if h <= left_count else [right]), result

    mine, theirs = [own], [swap(own, row_count)]
    acc, folded = None, 0

    def snaps_until(end, acc):
        blocks = [[whole_block(u) for u in some[folded:end]] for some in (mine, theirs)]
        return snap_product(inverse, *blocks, chips, folded, core, acc)

    def under_snaps(h, held):
        nonlocal acc, folded
        if h == 1:
            return steer(held)
        acc, folded = snaps_until(ends[h - 1], acc), ends[h - 1]
        return acc

    for h, group, result in travel(own, under_snaps):
        if h == 1:
            steered.append(result[0])
            powers.append(result[1])
        else:
            acc = result
        mine += group
        theirs += [swap(u, row_count) for u in group]
    local = snaps_until(len(mine), acc)

    sent = lax.optimization_barrier(local.astype(jnp.float16))
    wide = [sent.astype(f32)]
    coarse, fine = tables[1][:2]
    acc, folded = None, 0
    power, stride = None, 1

    def cross_until(end, acc):
        return cross_products(
            [whole_block(u) for u in mine[folded:end]],
            [whole_block(q) for q in wide[folded:end]],
            chips,
            folded,
            core,
            coarse,
            fine,
            acc,
        )

    def under_products(h, held):
        nonlocal acc, folded
        if h == 1:
            return steer(held)
        moved = exchange(power, stride, row_count)
        acc, folded = cross_until(ends[h - 1], acc), ends[h - 1]
        return acc, moved

    for h, group, result in travel(sent, under_products):
        if h == 1:
            steered.append(result[0])
            powers.append(result[1])
            power = jnp.concatenate(powers, 0)
            if row_count & (row_count - 1):
                power = lax.psum(power, "row")
        else:
            acc = result[0]
            power, stride = power + result[1], stride * 2
        wide += [q.astype(f32) for q in group]
    moved = exchange(power, stride, row_count)
    (kmat, bmat), moved = together(cross_until(len(mine), acc), moved)
    power, stride = power + moved, stride * 2
    while stride < row_count:
        power, stride = power + exchange(power, stride, row_count), stride * 2
    kmats, bmats = (kmat, swap(kmat, row_count)), (bmat, swap(bmat, row_count))
    x, second, fold = solve(float(window), kmats, bmats, local, steered[1])
    wide_theirs = [swap(q, row_count) for q in wide]
    power = jnp.concatenate([power[:1], power[1:] - fold], 0)
    spectrum = length / power
    new_inverse, weights = update(
        inverse,
        x,
        [whole_block(q) for q in wide],
        [whole_block(q) for q in wide_theirs],
        chips,
        core,
        (steered[0], second),
        spectrum,
    )
    return new_inverse, weights.reshape(STEPS, 2, rows, dirs), spectrum


def solution(mesh):
    row_count = mesh.shape["row"]
    in_specs = (
        P("groups", "row", None),
        P("groups", "row", None),
        P("groups", None, "row", None),
        P("groups", None),
        P("groups", None),
    )
    out_specs = (P("groups", "row", None), P("groups", None, "row", None), P("groups", None))
    return jax.shard_map(
        lambda *args: on_device(row_count, *args), mesh=mesh, in_specs=in_specs, out_specs=out_specs, check_vma=False
    )
```

```python
import jax
import jax.numpy as jnp
from jax import lax
from jax.experimental import pallas as pl
from jax.experimental.pallas import tpu as pltpu
from jax.sharding import PartitionSpec as P

STEPS = 2

f32 = jnp.float32
bf16 = jnp.bfloat16
HIGHEST = lax.Precision.HIGHEST
LANES = 128


def split(x):
    high = x.astype(bf16)
    return high, (x - high.astype(f32)).astype(bf16)


def mm(left, right):
    return jnp.dot(left, right, preferred_element_type=f32)


def mm_tn(left, right):
    return lax.dot_general(left, right, (((0,), (0,)), ((), ())), preferred_element_type=f32)


def mm_nt(left, right):
    return lax.dot_general(left, right, (((1,), (1,)), ((), ())), preferred_element_type=f32)


def exact(left, right, dims=((1,), (0,))):
    return lax.dot_general(left, right, (dims, ((), ())), precision=HIGHEST, preferred_element_type=f32)


def ring_order(row_count):
    chips = row_count // 2
    return list(range(0, chips, 2)) + list(reversed(range(1, chips, 2)))


def hop(block, row_count, shift):
    order = ring_order(row_count)
    chips = len(order)
    pairs = [(order[i] * 2 + core, order[(i + shift) % chips] * 2 + core) for i in range(chips) for core in range(2)]
    return lax.ppermute(block, "row", pairs)


def swap(block, row_count):
    return lax.ppermute(block, "row", [(i, i ^ 1) for i in range(row_count)])


def ring_counts(row_count):
    chips = row_count // 2
    right = chips // 2
    return right, chips - 1 - right


def together(*trees):
    return lax.optimization_barrier(trees)


def ring_chips(row_count):
    order = ring_order(row_count)
    chips = len(order)
    position = [0] * chips
    for place, chip in enumerate(order):
        position[chip] = place
    here = jnp.asarray(position, jnp.int32)[lax.axis_index("row") // 2]
    right, left = ring_counts(row_count)
    shifts, ends = [0], [1]
    for h in range(1, right + 1):
        shifts += [-h, h] if h <= left else [-h]
        ends.append(len(shifts))
    return jnp.asarray(order, jnp.int32)[(here + jnp.asarray(shifts, jnp.int32)) % chips], ends


def exchange(x, stride, row_count):
    if stride >= row_count or row_count & (row_count - 1):
        return jnp.zeros_like(x)
    return lax.ppermute(x, "row", [(i, i ^ stride) for i in range(row_count)])


def steering_tables(directions, length, inner):
    odd = 2 * directions[None, :] + 1 - 2 * length
    halves = jnp.concatenate(
        [
            jnp.arange(length // inner, dtype=jnp.int32) * (2 * inner),
            jnp.arange(inner, dtype=jnp.int32) * 2,
            jnp.arange(inner, dtype=jnp.int32) * 2 + 1,
            jnp.full((8,), length - 1, jnp.int32),
        ]
    )
    turns = (halves[:, None] * odd) % (8 * length)
    phase = jnp.pi * turns.astype(f32) / (4 * length)
    table = jnp.stack([jnp.cos(phase), jnp.sin(phase)])
    at = length // inner
    return table[:, :at], table[:, at : at + inner], table[:, at + inner : at + 2 * inner], table[:, at + 2 * inner :]


def steer_rows(coarse_ref, fine_ref, index):
    er, ei = coarse_ref[0, pl.ds(index, 1), :], coarse_ref[1, pl.ds(index, 1), :]
    fr, fi = fine_ref[0], fine_ref[1]
    return er * fr - ei * fi, er * fi + ei * fr


def embed(re, im):
    return jnp.concatenate([jnp.concatenate([re, -im], 1), jnp.concatenate([im, re], 1)], 0)


def steer_kernel(first_ref, right_ref, left_ref, coarse_ref, fine_ref, shifted_ref, centre_ref, h_ref, power_ref, *scratch):
    step = pl.program_id(0)
    rows, width = right_ref.shape[1], right_ref.shape[2]
    inner, dirs = fine_ref.shape[1], fine_ref.shape[2]
    a_high, a_low, flip = scratch
    count = width // inner
    side = flip.shape[0]

    @pl.when(step == 0)
    def _():
        row = lax.broadcasted_iota(jnp.int32, (side, side), 0)
        flip[...] = (row + lax.broadcasted_iota(jnp.int32, (side, side), 1) == side - 1).astype(f32).astype(bf16)

    for a in range(count):
        ar, ai = steer_rows(coarse_ref, shifted_ref, step * count + a)
        top, low = slice(a * inner, (a + 1) * inner), slice(width + a * inner, width + (a + 1) * inner)
        a_high[top, :], a_low[top, :] = split(ar)
        a_high[low, :], a_low[low, :] = split(ai)
    left = left_ref[...].reshape(2 * rows, width)
    stack = jnp.concatenate(split(left), 0)
    pieces = []
    for start in range(width - side, -1, -side):
        turned = mm(stack[:, start : start + side], flip[...])
        pieces.append(turned[: 2 * rows] + turned[2 * rows :])
    left = jnp.concatenate(pieces, 1)
    right = right_ref[...].reshape(2 * rows, width)
    even_high, even_low = split(right + left)
    odd_high, odd_low = split(right - left)

    def combined(even, odd):
        turned = jnp.concatenate([-odd[rows:], odd[:rows]], 0)
        return jnp.concatenate([even, turned], 1)

    high = combined(even_high, odd_high)
    part = mm(high, a_high[...]) + mm(combined(even_low, odd_low), a_high[...]) + mm(high, a_low[...])

    @pl.when(step == 0)
    def _():
        h_ref[...] = part

    @pl.when(step > 0)
    def _():
        h_ref[...] += part

    @pl.when(step == pl.num_programs(0) - 1)
    def _():
        re, im = h_ref[:rows, :], h_ref[rows:, :]
        cr, ci = centre_ref[0, :1, :], centre_ref[1, :1, :]
        h_ref[:rows, :] = re * cr - im * ci
        h_ref[rows:, :] = re * ci + im * cr

        def add(a, power):
            ar, ai = steer_rows(coarse_ref, fine_ref, first_ref[0] + a)
            top = pl.ds(pl.multiple_of(a * inner, inner), inner)
            low = pl.ds(pl.multiple_of(rows + a * inner, inner), inner)
            return power + jnp.sum(ar * h_ref[top, :] + ai * h_ref[low, :], axis=0, keepdims=True)

        power_ref[...] = lax.fori_loop(0, rows // inner, add, jnp.zeros((1, dirs), f32))


def steer_product(inverse, tables, first):
    _, rows, length = inverse.shape
    dirs = tables[0].shape[2]
    width = min(512, length // 2)
    steps = length // 2 // width
    side = min(2 * LANES, width)
    whole = lambda k, s: (0, 0)
    return pl.pallas_call(
        steer_kernel,
        grid_spec=pltpu.PrefetchScalarGridSpec(
            num_scalar_prefetch=1,
            grid=(steps,),
            in_specs=[
                pl.BlockSpec((2, rows, width), lambda k, s: (0, 0, steps + k)),
                pl.BlockSpec((2, rows, width), lambda k, s: (0, 0, steps - 1 - k)),
            ]
            + [pl.BlockSpec(t.shape, lambda k, s: (0, 0, 0)) for t in tables],
            out_specs=[pl.BlockSpec((2 * rows, dirs), whole), pl.BlockSpec((1, dirs), whole)],
            scratch_shapes=[
                pltpu.VMEM((2 * width, dirs), bf16),
                pltpu.VMEM((2 * width, dirs), bf16),
                pltpu.VMEM((side, side), bf16),
            ],
        ),
        out_shape=[jax.ShapeDtypeStruct((2 * rows, dirs), f32), jax.ShapeDtypeStruct((1, dirs), f32)],
        compiler_params=pltpu.CompilerParams(vmem_limit_bytes=24 << 20),
        name="steer",
    )(first, inverse, inverse, *tables)


def whole_block(array):
    return ((array, 0), (array, array.shape[0] // 2))


def each_array(block, apply):
    made = {}
    for array, _ in block:
        if id(array) not in made:
            made[id(array)] = apply(array)
    return tuple((made[id(array)], row) for array, row in block)


def arrays_of(blocks):
    arrays, places = [], {}
    for block in blocks:
        for array, _ in block:
            if id(array) not in places:
                places[id(array)] = len(arrays)
                arrays.append(array)
    return arrays, [tuple((places[id(array)], row) for array, row in block) for block in blocks]


def stream(step, plan, refs, buf, sem, where):
    def copies(g, slot):
        out = []
        for k, block in enumerate(plan[g]):
            for plane, (array, row) in enumerate(block):
                start, rows = where(k, plane)
                source = refs[array].at[pl.ds(row, rows), :]
                out.append(pltpu.make_async_copy(source, buf.at[slot, pl.ds(start, rows), :], sem.at[slot]))
        return out

    @pl.when(step == 0)
    def _():
        for c in copies(0, 0):
            c.start()

    for g in range(1, len(plan)):

        @pl.when(step + 1 == g)
        def _(g=g):
            for c in copies(g, g % 2):
                c.start()

    slot = step % 2
    pltpu.make_async_copy(buf.at[slot], buf.at[slot], sem.at[slot]).wait()
    return slot


def snap_kernel(plan, has_acc, chip_ref, core_ref, p_ref, *refs):
    out_ref, buf, sem = refs[-3:]
    step = pl.program_id(0)
    rows = p_ref.shape[1]
    core = core_ref[0]

    def where(k, plane):
        return pl.multiple_of((2 * plane + (core if k == 0 else 1 - core)) * rows, rows), rows

    slot = stream(step, plan, refs, buf, sem, where)
    re_high, re_low = split(p_ref[0])
    im_high, im_low = split(p_ref[1])
    snaps = buf[slot]
    part = mm(embed(re_high, im_high), snaps) + mm(embed(re_low, im_low), snaps)

    @pl.when(step == 0)
    def _():
        out_ref[...] = part + refs[-4][...] if has_acc else part

    @pl.when(step > 0)
    def _():
        out_ref[...] += part


def snap_product(inverse, mine, theirs, chips, begin, core, acc):
    _, rows, _ = inverse.shape
    arrays, plan = arrays_of(mine + theirs)
    count = len(mine)
    plan = [[plan[g], plan[count + g]] for g in range(count)]
    width = arrays[0].shape[1]
    whole = lambda *_: (0, 0)
    specs = [pl.BlockSpec((2, rows, 2 * rows), lambda i, s, c: (0, 0, s[begin + i]))]
    specs += [pl.BlockSpec(memory_space=pltpu.HBM)] * len(arrays)
    args = [inverse] + arrays
    if acc is not None:
        specs.append(pl.BlockSpec((2 * rows, width), whole))
        args.append(acc)
    return pl.pallas_call(
        lambda *refs: snap_kernel(plan, acc is not None, *refs),
        grid_spec=pltpu.PrefetchScalarGridSpec(
            num_scalar_prefetch=2,
            grid=(count,),
            in_specs=specs,
            out_specs=pl.BlockSpec((2 * rows, width), whole),
            scratch_shapes=[pltpu.VMEM((2, 4 * rows, width), bf16), pltpu.SemaphoreType.DMA((2,))],
        ),
        out_shape=jax.ShapeDtypeStruct((2 * rows, width), f32),
        compiler_params=pltpu.CompilerParams(vmem_limit_bytes=24 << 20),
        name="snaps",
    )(chips, core, *args)


def panels(width):
    offsets, at = [], 0
    for start in range(0, width, 2 * LANES):
        offsets.append(at)
        at += width - start
    return offsets, at


def cross_kernel(u_plan, q_plan, u_count, q_count, has_acc, begin, chip_ref, core_ref, coarse_ref, fine_ref, *refs):
    u_refs, q_refs = refs[:u_count], refs[u_count : u_count + q_count]
    k_ref, b_ref, u_buf, q_buf, a_high, a_low, u_sem, q_sem = refs[-8:]
    step = pl.program_id(0)
    rows, width = u_buf.shape[1] // 2, u_buf.shape[2]

    def where(k, plane):
        return plane * rows, rows

    u_slot = stream(step, u_plan, u_refs, u_buf, u_sem, where)
    q_slot = stream(step, q_plan, q_refs, q_buf, q_sem, where)
    inner, dirs = fine_ref.shape[1], fine_ref.shape[2]
    source = chip_ref[begin + step] * 2 + core_ref[0]
    for a in range(rows // inner):
        ar, ai = steer_rows(coarse_ref, fine_ref, source * (rows // inner) + a)
        top, low = slice(a * inner, (a + 1) * inner), slice(rows + a * inner, rows + (a + 1) * inner)
        re, im = split(ar), split(ai)
        for ref, r, i in ((a_high, re[0], im[0]), (a_low, re[1], im[1])):
            ref[top, :dirs], ref[low, :dirs] = r, i
            ref[top, dirs:], ref[low, dirs:] = i, -r

    q_high, q_low = split(q_buf[q_slot])
    first_high, first_low = q_high[:, : width // 2], q_low[:, : width // 2]
    b_part = mm_tn(first_high, a_high[...]) + mm_tn(first_low, a_high[...]) + mm_tn(first_high, a_low[...])
    snaps = u_buf[u_slot]
    parts = []
    for start in range(0, width, 2 * LANES):
        left = snaps[:, start:]
        part = None
        for q in (q_high, q_low):
            re, im = q[:rows, start : start + 2 * LANES], q[rows:, start : start + 2 * LANES]
            piece = mm_tn(left, jnp.concatenate([jnp.concatenate([re, im], 1), jnp.concatenate([im, -re], 1)], 0))
            part = piece if part is None else part + piece
        parts.append(part)
    offsets, total = panels(width)
    ends = offsets[1:] + [total]

    @pl.when(step == 0)
    def _():
        b_ref[...] = b_part + refs[-9][...] if has_acc else b_part
        for at, end, part in zip(offsets, ends, parts):
            k_ref[at:end, :] = part + refs[-10][at:end, :] if has_acc else part

    @pl.when(step > 0)
    def _():
        b_ref[...] += b_part
        for at, end, part in zip(offsets, ends, parts):
            k_ref[at:end, :] += part


def cross_products(snaps, products, chips, begin, core, coarse, fine, acc):
    u_arrays, u_plan = arrays_of(snaps)
    q_arrays, q_plan = arrays_of(products)
    u_plan, q_plan = [[u] for u in u_plan], [[q] for q in q_plan]
    width = u_arrays[0].shape[1]
    height = coarse.shape[1] * fine.shape[1] * 2 // (chips.shape[0] * 2)
    count = len(snaps)
    dirs = coarse.shape[2]
    whole = lambda *_: (0, 0)
    shapes = [(panels(width)[1], 4 * LANES), (width // 2, 2 * dirs)]
    specs = [pl.BlockSpec(coarse.shape, lambda *_: (0, 0, 0)), pl.BlockSpec(fine.shape, lambda *_: (0, 0, 0))]
    specs += [pl.BlockSpec(memory_space=pltpu.HBM)] * len(u_arrays) + [pl.BlockSpec(memory_space=pl.ANY)] * len(q_arrays)
    args = [coarse, fine] + u_arrays + q_arrays
    if acc is not None:
        specs += [pl.BlockSpec(s, whole) for s in shapes]
        args += list(acc)
    return pl.pallas_call(
        lambda *refs: cross_kernel(u_plan, q_plan, len(u_arrays), len(q_arrays), acc is not None, begin, *refs),
        grid_spec=pltpu.PrefetchScalarGridSpec(
            num_scalar_prefetch=2,
            grid=(count,),
            in_specs=specs,
            out_specs=[pl.BlockSpec(s, whole) for s in shapes],
            scratch_shapes=[
                pltpu.VMEM((2, height, width), bf16),
                pltpu.VMEM((2, height, width), f32),
                pltpu.VMEM((height, 2 * dirs), bf16),
                pltpu.VMEM((height, 2 * dirs), bf16),
                pltpu.SemaphoreType.DMA((2,)),
                pltpu.SemaphoreType.DMA((2,)),
            ],
        ),
        out_shape=[jax.ShapeDtypeStruct(s, f32) for s in shapes],
        compiler_params=pltpu.CompilerParams(vmem_limit_bytes=24 << 20),
        name="cross",
    )(chips, core, *args)


def near(left, right, dims=((1,), (0,))):
    left_high, left_low = split(left)
    right_high, right_low = split(right)
    dot = lambda a, b: lax.dot_general(a, b, (dims, ((), ())), preferred_element_type=f32)
    return dot(left_high, right_high) + dot(left_low, right_high) + dot(left_high, right_low)


def eye(n):
    return (lax.broadcasted_iota(jnp.int32, (n, n), 0) == lax.broadcasted_iota(jnp.int32, (n, n), 1)).astype(f32)


def spd_inverse(matrix, x_ref):
    n = matrix.shape[0]
    ident = eye(n)
    norm = jnp.max(jnp.sum(jnp.abs(matrix), axis=0, keepdims=True))
    begin = 1.9 / norm
    coarse = matrix.astype(bf16)
    x_ref[...] = ident * begin

    def rough(state):
        size, _, count = state
        x = x_ref[...]
        narrow = x.astype(bf16)
        r = ident - mm(coarse, narrow)
        x_ref[...] = x + mm(narrow, r.astype(bf16))
        return jnp.sum(r * r), size, count + 1

    def rough_more(state):
        size, last, count = state
        return jnp.logical_and(size > 0.05, jnp.logical_and(size < last, count < 32))

    huge = jnp.float32(3e38)
    size, _, _ = lax.while_loop(rough_more, rough, (huge / 2, huge, 0))

    @pl.when(jnp.logical_not(size < 0.25))
    def _():
        x_ref[...] = ident * begin

    def fine(state):
        size, _, count = state
        x = x_ref[...]
        r = ident - exact(matrix, x)
        x_ref[...] = x + near(x, r)
        return jnp.sum(r * r), size, count + 1

    def fine_more(state):
        size, last, count = state
        moving = jnp.logical_or(size > 0.25, size < 0.5 * last)
        return jnp.logical_and(size > 1e-5, jnp.logical_and(moving, count < 64))

    lax.while_loop(fine_more, fine, (huge / 4, huge, 0))
    x = x_ref[...]
    return 0.5 * (x + x.T)


def quasi_inverse(block, x_ref):
    a, c, b = block(0, 0), block(1, 0), block(1, 1)
    first = spd_inverse(0.5 * (a + a.T), x_ref)
    v = near(first, c, ((1,), (1,)))
    schur = near(c, v) - b
    second = spd_inverse(0.5 * (schur + schur.T), x_ref)
    cross = near(v, second)
    corner = first - near(cross, v, ((1,), (1,)))
    n = LANES
    re = jnp.concatenate(
        [
            jnp.concatenate([corner[:n, :n], cross[:n, :n]], 1),
            jnp.concatenate([cross[:n, :n].T, -second[:n, :n]], 1),
        ],
        0,
    )
    im = jnp.concatenate(
        [
            jnp.concatenate([corner[n:, :n], cross[n:, :n]], 1),
            jnp.concatenate([-cross[n:, :n].T, -second[n:, :n]], 1),
        ],
        0,
    )
    return re, im


def solve_kernel(window, k_ref, k_more, b_any, b_more_any, q_any, h_any, x_ref, h_out, power_ref, *scratch):
    s_re, s_im, newton, b_ref, b_more, q_ref, h_ref, sem = scratch
    pairs = ((q_any, q_ref), (b_any, b_ref), (b_more_any, b_more), (h_any, h_ref))
    late = [pltpu.make_async_copy(source, target, sem.at[i]) for i, (source, target) in enumerate(pairs)]
    for copy in late:
        copy.start()
    rows, width = q_ref.shape[0] // 2, q_ref.shape[1]
    half = width // 2
    offsets, _ = panels(width)

    def tile(p, q):
        at = offsets[q // 2] + (p - q // 2 * 2) * LANES
        m = k_ref[at : at + LANES, :] + k_more[at : at + LANES, :]
        start = (q % 2) * LANES
        return m[:, start : start + LANES], m[:, 2 * LANES + start : 3 * LANES + start]

    def diagonal(p):
        return (window if p % 2 == 0 else -window) * eye(2 * LANES)

    def first_block(p, q):
        e = embed(*tile(p, q))
        return e + diagonal(p) if p == q else e

    g_re, g_im = quasi_inverse(first_block, newton)
    k21 = [[tile(p, q) for q in (0, 1)] for p in (2, 3)]
    k21_re = jnp.concatenate([jnp.concatenate([t[0] for t in line], 1) for line in k21], 0)
    k21_im = jnp.concatenate([jnp.concatenate([t[1] for t in line], 1) for line in k21], 0)
    g_emb = embed(g_re, g_im)
    w = near(g_emb, jnp.concatenate([k21_re.T, -k21_im.T], 0))
    w_re, w_im = w[:half], w[half:]
    fold = near(embed(k21_re, k21_im), w)
    s_re[...], s_im[...] = fold[:half], fold[half:]

    def second_block(p, q):
        at, to = slice(p * LANES, (p + 1) * LANES), slice(q * LANES, (q + 1) * LANES)
        re, im = tile(p + 2, q + 2)
        e = embed(re - s_re[at, to], im - s_im[at, to])
        return e + diagonal(p) if p == q else e

    i_re, i_im = quasi_inverse(second_block, newton)
    for copy in late:
        copy.wait()
    q1 = jnp.concatenate([q_ref[:rows, :half], q_ref[rows:, :half]], 1)
    q2 = jnp.concatenate([q_ref[:rows, half:], q_ref[rows:, half:]], 1)
    y = near(q1, embed(g_re, -g_im))
    x2 = near(q2 - near(q1, embed(w_re, -w_im)), embed(i_re, -i_im))
    x1 = y - near(x2, embed(w_re.T, w_im.T))
    x_ref[:, :half], x_ref[:, half:width] = x1[:, :half], x2[:, :half]
    x_ref[:, width : width + half], x_ref[:, width + half :] = x1[:, half:], x2[:, half:]
    dirs = h_ref.shape[1]
    b = b_ref[...] + b_more[...]
    b = jnp.concatenate([b[:, :dirs], b[:, dirs:]], 0)
    gb = near(g_emb, b)
    power_ref[...] = jnp.sum(b * gb, axis=0, keepdims=True)
    h_out[...] = h_ref[...] - near(embed(q_ref[:rows, :half], q_ref[rows:, :half]), gb)


def solve(window, kmats, bmats, local, h):
    width = local.shape[1]
    rows, dirs = h.shape[0] // 2, h.shape[1]
    return pl.pallas_call(
        lambda *refs: solve_kernel(window, *refs),
        out_shape=[
            jax.ShapeDtypeStruct((rows, 2 * width), f32),
            jax.ShapeDtypeStruct(h.shape, f32),
            jax.ShapeDtypeStruct((1, dirs), f32),
        ],
        in_specs=[pl.BlockSpec(memory_space=pltpu.VMEM)] * 2 + [pl.BlockSpec(memory_space=pl.ANY)] * 4,
        scratch_shapes=[pltpu.VMEM((width // 2, width // 2), f32)] * 2
        + [pltpu.VMEM((2 * LANES, 2 * LANES), f32)]
        + [pltpu.VMEM(a.shape, f32) for a in (*bmats, local, h)]
        + [pltpu.SemaphoreType.DMA((4,))],
        compiler_params=pltpu.CompilerParams(vmem_limit_bytes=28 << 20),
        name="solve",
    )(*kmats, *bmats, local, h)


def update_kernel(plan, chip_ref, core_ref, p_ref, x_ref, h0_ref, h1_ref, scale_ref, *refs):
    out_ref, weight_ref, buf, x_high, x_low, sem = refs[-6:]
    step = pl.program_id(0)
    rows = p_ref.shape[1]
    width = x_ref.shape[1] // 2
    core = core_ref[0]

    @pl.when(step == 0)
    def _():
        high, low = split(x_ref[...])
        for ref, v in ((x_high, high), (x_low, low)):
            ref[:rows, :] = v
            ref[rows:, :width], ref[rows:, width:] = v[:, width:], -v[:, :width]

    def where(k, plane):
        return pl.multiple_of((2 * plane + (core if k == 0 else 1 - core)) * rows, rows), rows

    slot = stream(step, plan, refs, buf, sem, where)
    q_high, q_low = split(jnp.concatenate([buf[slot, : 2 * rows, :], buf[slot, 2 * rows :, :]], 1))
    part = mm_nt(x_high[...], q_high) + mm_nt(x_low[...], q_high) + mm_nt(x_high[...], q_low)
    out_ref[0] = p_ref[0] - part[:rows]
    out_ref[1] = p_ref[1] - part[rows:]
    weight_ref[0] = h0_ref[...] * scale_ref[:1, :]
    weight_ref[1] = h1_ref[...] * scale_ref[1:2, :]


def update(inverse, x, mine, theirs, chips, core, steered, scale):
    _, rows, length = inverse.shape
    width = x.shape[1] // 2
    arrays, plan = arrays_of(mine + theirs)
    count = len(mine)
    plan = [[plan[g], plan[count + g]] for g in range(count)]
    dirs = scale.shape[1]
    piece = 2 * rows // count
    return pl.pallas_call(
        lambda *refs: update_kernel(plan, *refs),
        grid_spec=pltpu.PrefetchScalarGridSpec(
            num_scalar_prefetch=2,
            grid=(count,),
            in_specs=[
                pl.BlockSpec((2, rows, 2 * rows), lambda i, s, c: (0, 0, s[i])),
                pl.BlockSpec((rows, 2 * width), lambda i, s, c: (0, 0)),
                pl.BlockSpec((piece, dirs), lambda i, s, c: (i, 0)),
                pl.BlockSpec((piece, dirs), lambda i, s, c: (i, 0)),
                pl.BlockSpec(scale.shape, lambda i, s, c: (0, 0)),
            ]
            + [pl.BlockSpec(memory_space=pl.ANY)] * len(arrays),
            out_specs=[
                pl.BlockSpec((2, rows, 2 * rows), lambda i, s, c: (0, 0, s[i])),
                pl.BlockSpec((2, piece, dirs), lambda i, s, c: (0, i, 0)),
            ],
            scratch_shapes=[
                pltpu.VMEM((2, 4 * rows, width), f32),
                pltpu.VMEM((2 * rows, 2 * width), bf16),
                pltpu.VMEM((2 * rows, 2 * width), bf16),
                pltpu.SemaphoreType.DMA((2,)),
            ],
        ),
        out_shape=[jax.ShapeDtypeStruct(inverse.shape, f32), jax.ShapeDtypeStruct((2, 2 * rows, dirs), f32)],
        compiler_params=pltpu.CompilerParams(vmem_limit_bytes=28 << 20),
        name="update",
    )(chips, core, inverse, x, *steered, scale, *arrays)


def on_device(row_count, inverse, cycle, arrivals, departing, directions):
    rows, length = inverse.shape[1], inverse.shape[2]
    window = cycle.shape[2]
    snap = arrivals.shape[3]
    dirs = directions.shape[1]
    inner = 64
    me = lax.axis_index("row").astype(jnp.int32)
    first = (me * (rows // inner))[None]
    core = (me % 2)[None]
    chips, ends = ring_chips(row_count)
    right_count, left_count = ring_counts(row_count)

    slots = departing.reshape(-1)
    pick = (jnp.arange(window, dtype=jnp.int32)[:, None] == slots[None, :]).astype(bf16)
    departed = mm(cycle.reshape(2 * rows, window), pick).astype(bf16)
    blocks = []
    for t in range(STEPS):
        blocks += [arrivals[t].reshape(2 * rows, snap), departed[:, t * snap : (t + 1) * snap]]
    own = jnp.concatenate(blocks, 1)

    tables = [steering_tables(directions[t], length, inner) for t in range(STEPS)]
    steered, powers = [], []

    def steer(after):
        after, place = together(after, first)
        return steer_product(inverse, tables[len(steered)], place)

    def travel(block, work):
        right = left = block
        for h in range(1, right_count + 1):
            held = (right, left)
            if h <= left_count:
                moved = hop(right, row_count, 1), hop(left, row_count, -1)
            elif right_count > left_count:
                moved = hop(right[:rows], row_count, 1), hop(left[rows:], row_count, -1)
            (right, left), result = together(moved, work(h, held))
            group = [whole_block(right), whole_block(left)] if h <= left_count else [((right, 0), (left, 0))]
            yield h, group, result

    mine, theirs = [whole_block(own)], [whole_block(swap(own, row_count))]
    acc, folded = None, 0

    def snaps_until(end, acc):
        return snap_product(inverse, mine[folded:end], theirs[folded:end], chips, folded, core, acc)

    def under_snaps(h, held):
        nonlocal acc, folded
        if h == 1:
            return together(tables, held)[0]
        if h == 2:
            return steer(held)
        acc, folded = snaps_until(ends[h - 1], acc), ends[h - 1]
        return acc

    for h, group, result in travel(own, under_snaps):
        if h == 1:
            tables = result
        elif h == 2:
            steered.append(result[0])
            powers.append(result[1])
        else:
            acc = result
        mine += group
        theirs += [each_array(u, lambda v: swap(v, row_count)) for u in group]
    local = snaps_until(len(mine), acc)

    sent = lax.optimization_barrier(local.astype(jnp.float16))
    wide = [whole_block(sent.astype(f32))]
    coarse, fine = tables[1][:2]
    acc, folded = None, 0
    power, stride = None, 1

    def cross_until(end, acc):
        return cross_products(mine[folded:end], wide[folded:end], chips, folded, core, coarse, fine, acc)

    def under_products(h, held):
        nonlocal acc, folded
        if h == 1:
            return steer(held)
        moved = exchange(power, stride, row_count)
        if h < right_count:
            acc, folded = cross_until(ends[h - 1], acc), ends[h - 1]
        return acc, moved

    for h, group, result in travel(sent, under_products):
        if h == 1:
            steered.append(result[0])
            powers.append(result[1])
            power = jnp.concatenate(powers, 0)
            if row_count & (row_count - 1):
                power = lax.psum(power, "row")
        else:
            acc, moved = result
            power, stride = power + moved, stride * 2
        wide += [each_array(q, lambda v: v.astype(f32)) for q in group]
    moved = exchange(power, stride, row_count)
    (kmat, bmat), moved = together(cross_until(len(mine), acc), moved)
    power, stride = power + moved, stride * 2
    while stride < row_count:
        power, stride = power + exchange(power, stride, row_count), stride * 2
    kmats, bmats = (kmat, swap(kmat, row_count)), (bmat, swap(bmat, row_count))

    x, second, fold = solve(float(window), kmats, bmats, local, steered[1])
    wide_theirs = [each_array(q, lambda v: swap(v, row_count)) for q in wide]
    power = jnp.concatenate([power[:1], power[1:] - fold], 0)
    spectrum = length / power
    new_inverse, weights = update(
        inverse,
        x,
        wide,
        wide_theirs,
        chips,
        core,
        (steered[0], second),
        spectrum,
    )
    return new_inverse, weights.reshape(STEPS, 2, rows, dirs), spectrum


def solution(mesh):
    row_count = mesh.shape["row"]
    in_specs = (
        P("groups", "row", None),
        P("groups", "row", None),
        P("groups", None, "row", None),
        P("groups", None),
        P("groups", None),
    )
    out_specs = (P("groups", "row", None), P("groups", None, "row", None), P("groups", None))
    return jax.shard_map(
        lambda *args: on_device(row_count, *args), mesh=mesh, in_specs=in_specs, out_specs=out_specs, check_vma=False
    )
```

```python
import jax
import jax.numpy as jnp
from jax import lax
from jax.experimental import pallas as pl
from jax.experimental.pallas import tpu as pltpu
from jax.sharding import PartitionSpec as P

STEPS = 2

f32 = jnp.float32
bf16 = jnp.bfloat16
HIGHEST = lax.Precision.HIGHEST
LANES = 128


def split(x):
    high = x.astype(bf16)
    return high, (x - high.astype(f32)).astype(bf16)


def mm(left, right):
    return jnp.dot(left, right, preferred_element_type=f32)


def mm_tn(left, right):
    return lax.dot_general(left, right, (((0,), (0,)), ((), ())), preferred_element_type=f32)


def mm_nt(left, right):
    return lax.dot_general(left, right, (((1,), (1,)), ((), ())), preferred_element_type=f32)


def exact(left, right, dims=((1,), (0,))):
    return lax.dot_general(left, right, (dims, ((), ())), precision=HIGHEST, preferred_element_type=f32)


def ring_order(row_count):
    chips = row_count // 2
    return list(range(0, chips, 2)) + list(reversed(range(1, chips, 2)))


def hop(block, row_count, shift):
    order = ring_order(row_count)
    chips = len(order)
    pairs = [(order[i] * 2 + core, order[(i + shift) % chips] * 2 + core) for i in range(chips) for core in range(2)]
    return lax.ppermute(block, "row", pairs)


def swap(block, row_count):
    return lax.ppermute(block, "row", [(i, i ^ 1) for i in range(row_count)])


def ring_counts(row_count):
    chips = row_count // 2
    right = chips // 2
    return right, chips - 1 - right


def together(*trees):
    return lax.optimization_barrier(trees)


def ring_chips(row_count):
    order = ring_order(row_count)
    chips = len(order)
    position = [0] * chips
    for place, chip in enumerate(order):
        position[chip] = place
    here = jnp.asarray(position, jnp.int32)[lax.axis_index("row") // 2]
    right, left = ring_counts(row_count)
    shifts, ends = [0], [1]
    for h in range(1, right + 1):
        shifts += [-h, h] if h <= left else [-h]
        ends.append(len(shifts))
    return jnp.asarray(order, jnp.int32)[(here + jnp.asarray(shifts, jnp.int32)) % chips], ends


def exchange(x, stride, row_count):
    if stride >= row_count or row_count & (row_count - 1):
        return jnp.zeros_like(x)
    return lax.ppermute(x, "row", [(i, i ^ stride) for i in range(row_count)])


def steering_tables(directions, length, inner):
    odd = 2 * directions[None, :] + 1 - 2 * length
    halves = jnp.concatenate(
        [
            jnp.arange(length // inner, dtype=jnp.int32) * (2 * inner),
            jnp.arange(inner, dtype=jnp.int32) * 2,
            jnp.arange(inner, dtype=jnp.int32) * 2 + 1,
            jnp.full((8,), length - 1, jnp.int32),
        ]
    )
    turns = (halves[:, None] * odd) % (8 * length)
    phase = jnp.pi * turns.astype(f32) / (4 * length)
    table = jnp.stack([jnp.cos(phase), jnp.sin(phase)])
    at = length // inner
    return table[:, :at], table[:, at : at + inner], table[:, at + inner : at + 2 * inner], table[:, at + 2 * inner :]


def steer_rows(coarse_ref, fine_ref, index):
    er, ei = coarse_ref[0, pl.ds(index, 1), :], coarse_ref[1, pl.ds(index, 1), :]
    fr, fi = fine_ref[0], fine_ref[1]
    return er * fr - ei * fi, er * fi + ei * fr


def embed(re, im):
    return jnp.concatenate([jnp.concatenate([re, -im], 1), jnp.concatenate([im, re], 1)], 0)


def steer_kernel(first_ref, right_ref, left_ref, coarse_ref, fine_ref, shifted_ref, centre_ref, h_ref, power_ref, *scratch):
    step = pl.program_id(0)
    rows, width = right_ref.shape[1], right_ref.shape[2]
    inner, dirs = fine_ref.shape[1], fine_ref.shape[2]
    a_high, a_low, flip = scratch
    count = width // inner
    side = flip.shape[0]

    @pl.when(step == 0)
    def _():
        row = lax.broadcasted_iota(jnp.int32, (side, side), 0)
        flip[...] = (row + lax.broadcasted_iota(jnp.int32, (side, side), 1) == side - 1).astype(f32).astype(bf16)

    for a in range(count):
        ar, ai = steer_rows(coarse_ref, shifted_ref, step * count + a)
        top, low = slice(a * inner, (a + 1) * inner), slice(width + a * inner, width + (a + 1) * inner)
        a_high[top, :], a_low[top, :] = split(ar)
        a_high[low, :], a_low[low, :] = split(ai)
    left = left_ref[...].reshape(2 * rows, width)
    stack = jnp.concatenate(split(left), 0)
    pieces = []
    for start in range(width - side, -1, -side):
        turned = mm(stack[:, start : start + side], flip[...])
        pieces.append(turned[: 2 * rows] + turned[2 * rows :])
    left = jnp.concatenate(pieces, 1)
    right = right_ref[...].reshape(2 * rows, width)
    even_high, even_low = split(right + left)
    odd_high, odd_low = split(right - left)

    def combined(even, odd):
        turned = jnp.concatenate([-odd[rows:], odd[:rows]], 0)
        return jnp.concatenate([even, turned], 1)

    high = combined(even_high, odd_high)
    part = mm(high, a_high[...]) + mm(combined(even_low, odd_low), a_high[...]) + mm(high, a_low[...])

    @pl.when(step == 0)
    def _():
        h_ref[...] = part

    @pl.when(step > 0)
    def _():
        h_ref[...] += part

    @pl.when(step == pl.num_programs(0) - 1)
    def _():
        re, im = h_ref[:rows, :], h_ref[rows:, :]
        cr, ci = centre_ref[0, :1, :], centre_ref[1, :1, :]
        h_ref[:rows, :] = re * cr - im * ci
        h_ref[rows:, :] = re * ci + im * cr

        def add(a, power):
            ar, ai = steer_rows(coarse_ref, fine_ref, first_ref[0] + a)
            top = pl.ds(pl.multiple_of(a * inner, inner), inner)
            low = pl.ds(pl.multiple_of(rows + a * inner, inner), inner)
            return power + jnp.sum(ar * h_ref[top, :] + ai * h_ref[low, :], axis=0, keepdims=True)

        power_ref[...] = lax.fori_loop(0, rows // inner, add, jnp.zeros((1, dirs), f32))


def steer_product(inverse, tables, first):
    _, rows, length = inverse.shape
    dirs = tables[0].shape[2]
    width = min(512, length // 2)
    steps = length // 2 // width
    side = min(2 * LANES, width)
    whole = lambda k, s: (0, 0)
    return pl.pallas_call(
        steer_kernel,
        grid_spec=pltpu.PrefetchScalarGridSpec(
            num_scalar_prefetch=1,
            grid=(steps,),
            in_specs=[
                pl.BlockSpec((2, rows, width), lambda k, s: (0, 0, steps + k)),
                pl.BlockSpec((2, rows, width), lambda k, s: (0, 0, steps - 1 - k)),
            ]
            + [pl.BlockSpec(t.shape, lambda k, s: (0, 0, 0)) for t in tables],
            out_specs=[pl.BlockSpec((2 * rows, dirs), whole), pl.BlockSpec((1, dirs), whole)],
            scratch_shapes=[
                pltpu.VMEM((2 * width, dirs), bf16),
                pltpu.VMEM((2 * width, dirs), bf16),
                pltpu.VMEM((side, side), bf16),
            ],
        ),
        out_shape=[jax.ShapeDtypeStruct((2 * rows, dirs), f32), jax.ShapeDtypeStruct((1, dirs), f32)],
        compiler_params=pltpu.CompilerParams(vmem_limit_bytes=56 << 20),
        name="steer",
    )(first, inverse, inverse, *tables)


def whole_block(array):
    return ((array, 0), (array, array.shape[0] // 2))


def each_array(block, apply):
    made = {}
    for array, _ in block:
        if id(array) not in made:
            made[id(array)] = apply(array)
    return tuple((made[id(array)], row) for array, row in block)


def arrays_of(blocks):
    arrays, places = [], {}
    for block in blocks:
        for array, _ in block:
            if id(array) not in places:
                places[id(array)] = len(arrays)
                arrays.append(array)
    return arrays, [tuple((places[id(array)], row) for array, row in block) for block in blocks]


def stream(step, plan, refs, buf, sem, where):
    def copies(g, slot):
        out = []
        for k, block in enumerate(plan[g]):
            for plane, (array, row) in enumerate(block):
                start, rows = where(k, plane)
                source = refs[array].at[pl.ds(row, rows), :]
                out.append(pltpu.make_async_copy(source, buf.at[slot, pl.ds(start, rows), :], sem.at[slot]))
        return out

    @pl.when(step == 0)
    def _():
        for c in copies(0, 0):
            c.start()

    for g in range(1, len(plan)):

        @pl.when(step + 1 == g)
        def _(g=g):
            for c in copies(g, g % 2):
                c.start()

    slot = step % 2
    pltpu.make_async_copy(buf.at[slot], buf.at[slot], sem.at[slot]).wait()
    return slot


def snap_kernel(plan, has_acc, chip_ref, core_ref, p_ref, *refs):
    out_ref, buf, sem = refs[-3:]
    step = pl.program_id(0)
    rows = p_ref.shape[1]
    core = core_ref[0]

    def where(k, plane):
        return pl.multiple_of((2 * plane + (core if k == 0 else 1 - core)) * rows, rows), rows

    slot = stream(step, plan, refs, buf, sem, where)
    re_high, re_low = split(p_ref[0])
    im_high, im_low = split(p_ref[1])
    snaps = buf[slot]
    part = mm(embed(re_high, im_high), snaps) + mm(embed(re_low, im_low), snaps)

    @pl.when(step == 0)
    def _():
        out_ref[...] = part + refs[-4][...] if has_acc else part

    @pl.when(step > 0)
    def _():
        out_ref[...] += part


def snap_product(inverse, mine, theirs, chips, begin, core, acc):
    _, rows, _ = inverse.shape
    arrays, plan = arrays_of(mine + theirs)
    count = len(mine)
    plan = [[plan[g], plan[count + g]] for g in range(count)]
    width = arrays[0].shape[1]
    whole = lambda *_: (0, 0)
    specs = [pl.BlockSpec((2, rows, 2 * rows), lambda i, s, c: (0, 0, s[begin + i]))]
    specs += [pl.BlockSpec(memory_space=pltpu.HBM)] * len(arrays)
    args = [inverse] + arrays
    if acc is not None:
        specs.append(pl.BlockSpec((2 * rows, width), whole))
        args.append(acc)
    return pl.pallas_call(
        lambda *refs: snap_kernel(plan, acc is not None, *refs),
        grid_spec=pltpu.PrefetchScalarGridSpec(
            num_scalar_prefetch=2,
            grid=(count,),
            in_specs=specs,
            out_specs=pl.BlockSpec((2 * rows, width), whole),
            scratch_shapes=[pltpu.VMEM((2, 4 * rows, width), bf16), pltpu.SemaphoreType.DMA((2,))],
        ),
        out_shape=jax.ShapeDtypeStruct((2 * rows, width), f32),
        compiler_params=pltpu.CompilerParams(vmem_limit_bytes=24 << 20),
        name="snaps",
    )(chips, core, *args)


def panels(width):
    offsets, at = [], 0
    for start in range(0, width, 2 * LANES):
        offsets.append(at)
        at += width - start
    return offsets, at


def cross_kernel(u_plan, q_plan, u_count, q_count, has_acc, begin, chip_ref, core_ref, coarse_ref, fine_ref, *refs):
    u_refs, q_refs = refs[:u_count], refs[u_count : u_count + q_count]
    k_ref, b_ref, u_buf, q_buf, a_high, a_low, u_sem, q_sem = refs[-8:]
    step = pl.program_id(0)
    rows, width = u_buf.shape[1] // 2, u_buf.shape[2]

    def where(k, plane):
        return plane * rows, rows

    u_slot = stream(step, u_plan, u_refs, u_buf, u_sem, where)
    q_slot = stream(step, q_plan, q_refs, q_buf, q_sem, where)
    inner, dirs = fine_ref.shape[1], fine_ref.shape[2]
    source = chip_ref[begin + step] * 2 + core_ref[0]
    for a in range(rows // inner):
        ar, ai = steer_rows(coarse_ref, fine_ref, source * (rows // inner) + a)
        top, low = slice(a * inner, (a + 1) * inner), slice(rows + a * inner, rows + (a + 1) * inner)
        re, im = split(ar), split(ai)
        for ref, r, i in ((a_high, re[0], im[0]), (a_low, re[1], im[1])):
            ref[top, :dirs], ref[low, :dirs] = r, i
            ref[top, dirs:], ref[low, dirs:] = i, -r

    q_high, q_low = split(q_buf[q_slot])
    first_high, first_low = q_high[:, : width // 2], q_low[:, : width // 2]
    b_part = mm_tn(first_high, a_high[...]) + mm_tn(first_low, a_high[...]) + mm_tn(first_high, a_low[...])
    snaps = u_buf[u_slot]
    parts = []
    for start in range(0, width, 2 * LANES):
        left = snaps[:, start:]
        part = None
        for q in (q_high, q_low):
            re, im = q[:rows, start : start + 2 * LANES], q[rows:, start : start + 2 * LANES]
            piece = mm_tn(left, jnp.concatenate([jnp.concatenate([re, im], 1), jnp.concatenate([im, -re], 1)], 0))
            part = piece if part is None else part + piece
        parts.append(part)
    offsets, total = panels(width)
    ends = offsets[1:] + [total]

    @pl.when(step == 0)
    def _():
        b_ref[...] = b_part + refs[-9][...] if has_acc else b_part
        for at, end, part in zip(offsets, ends, parts):
            k_ref[at:end, :] = part + refs[-10][at:end, :] if has_acc else part

    @pl.when(step > 0)
    def _():
        b_ref[...] += b_part
        for at, end, part in zip(offsets, ends, parts):
            k_ref[at:end, :] += part


def cross_products(snaps, products, chips, begin, core, coarse, fine, acc):
    u_arrays, u_plan = arrays_of(snaps)
    q_arrays, q_plan = arrays_of(products)
    u_plan, q_plan = [[u] for u in u_plan], [[q] for q in q_plan]
    width = u_arrays[0].shape[1]
    height = coarse.shape[1] * fine.shape[1] * 2 // (chips.shape[0] * 2)
    count = len(snaps)
    dirs = coarse.shape[2]
    whole = lambda *_: (0, 0)
    shapes = [(panels(width)[1], 4 * LANES), (width // 2, 2 * dirs)]
    specs = [pl.BlockSpec(coarse.shape, lambda *_: (0, 0, 0)), pl.BlockSpec(fine.shape, lambda *_: (0, 0, 0))]
    specs += [pl.BlockSpec(memory_space=pltpu.HBM)] * len(u_arrays) + [pl.BlockSpec(memory_space=pl.ANY)] * len(q_arrays)
    args = [coarse, fine] + u_arrays + q_arrays
    if acc is not None:
        specs += [pl.BlockSpec(s, whole) for s in shapes]
        args += list(acc)
    return pl.pallas_call(
        lambda *refs: cross_kernel(u_plan, q_plan, len(u_arrays), len(q_arrays), acc is not None, begin, *refs),
        grid_spec=pltpu.PrefetchScalarGridSpec(
            num_scalar_prefetch=2,
            grid=(count,),
            in_specs=specs,
            out_specs=[pl.BlockSpec(s, whole) for s in shapes],
            scratch_shapes=[
                pltpu.VMEM((2, height, width), bf16),
                pltpu.VMEM((2, height, width), f32),
                pltpu.VMEM((height, 2 * dirs), bf16),
                pltpu.VMEM((height, 2 * dirs), bf16),
                pltpu.SemaphoreType.DMA((2,)),
                pltpu.SemaphoreType.DMA((2,)),
            ],
        ),
        out_shape=[jax.ShapeDtypeStruct(s, f32) for s in shapes],
        compiler_params=pltpu.CompilerParams(vmem_limit_bytes=24 << 20),
        name="cross",
    )(chips, core, *args)


def near(left, right, dims=((1,), (0,))):
    left_high, left_low = split(left)
    right_high, right_low = split(right)
    dot = lambda a, b: lax.dot_general(a, b, (dims, ((), ())), preferred_element_type=f32)
    return dot(left_high, right_high) + dot(left_low, right_high) + dot(left_high, right_low)


def eye(n):
    return (lax.broadcasted_iota(jnp.int32, (n, n), 0) == lax.broadcasted_iota(jnp.int32, (n, n), 1)).astype(f32)


def spd_inverse(matrix, x_ref):
    n = matrix.shape[0]
    ident = eye(n)
    norm = jnp.max(jnp.sum(jnp.abs(matrix), axis=0, keepdims=True))
    begin = 1.9 / norm
    coarse = matrix.astype(bf16)
    x_ref[...] = ident * begin

    def rough(state):
        size, _, count = state
        x = x_ref[...]
        narrow = x.astype(bf16)
        r = ident - mm(coarse, narrow)
        x_ref[...] = x + mm(narrow, r.astype(bf16))
        return jnp.sum(r * r), size, count + 1

    def rough_more(state):
        size, last, count = state
        return jnp.logical_and(size > 0.05, jnp.logical_and(size < last, count < 32))

    huge = jnp.float32(3e38)
    size, _, _ = lax.while_loop(rough_more, rough, (huge / 2, huge, 0))

    @pl.when(jnp.logical_not(size < 0.25))
    def _():
        x_ref[...] = ident * begin

    def fine(state):
        size, _, count = state
        x = x_ref[...]
        r = ident - exact(matrix, x)
        x_ref[...] = x + near(x, r)
        return jnp.sum(r * r), size, count + 1

    def fine_more(state):
        size, last, count = state
        moving = jnp.logical_or(size > 0.25, size < 0.5 * last)
        return jnp.logical_and(size > 1e-5, jnp.logical_and(moving, count < 64))

    lax.while_loop(fine_more, fine, (huge / 4, huge, 0))
    x = x_ref[...]
    return 0.5 * (x + x.T)


def quasi_inverse(block, x_ref):
    a, c, b = block(0, 0), block(1, 0), block(1, 1)
    first = spd_inverse(0.5 * (a + a.T), x_ref)
    v = near(first, c, ((1,), (1,)))
    schur = near(c, v) - b
    second = spd_inverse(0.5 * (schur + schur.T), x_ref)
    cross = near(v, second)
    corner = first - near(cross, v, ((1,), (1,)))
    n = LANES
    re = jnp.concatenate(
        [
            jnp.concatenate([corner[:n, :n], cross[:n, :n]], 1),
            jnp.concatenate([cross[:n, :n].T, -second[:n, :n]], 1),
        ],
        0,
    )
    im = jnp.concatenate(
        [
            jnp.concatenate([corner[n:, :n], cross[n:, :n]], 1),
            jnp.concatenate([-cross[n:, :n].T, -second[n:, :n]], 1),
        ],
        0,
    )
    return re, im


def solve_kernel(window, k_ref, k_more, b_any, b_more_any, q_any, h_any, x_ref, h_out, power_ref, *scratch):
    s_re, s_im, newton, inv_ref, w_ref, b_ref, b_more, q_ref, h_ref, sem = scratch
    pairs = ((q_any, q_ref), (b_any, b_ref), (b_more_any, b_more), (h_any, h_ref))
    late = [pltpu.make_async_copy(source, target, sem.at[i]) for i, (source, target) in enumerate(pairs)]
    for copy in late:
        copy.start()
    rows, width = q_ref.shape[0] // 2, q_ref.shape[1]
    half = width // 2
    offsets, _ = panels(width)

    def tile(p, q):
        at = offsets[q // 2] + (p - q // 2 * 2) * LANES
        m = k_ref[at : at + LANES, :] + k_more[at : at + LANES, :]
        start = (q % 2) * LANES
        return m[:, start : start + LANES], m[:, 2 * LANES + start : 3 * LANES + start]

    def lines(p, q):
        tiles = [[tile(p + i, q + j) for j in (0, 1)] for i in (0, 1)]
        return [jnp.concatenate([jnp.concatenate([t[part] for t in line], 1) for line in tiles], 0) for part in (0, 1)]

    def load(p, less_re, less_im):
        for i in (0, 1):
            for j in range(i + 1):
                at, to = slice(i * LANES, (i + 1) * LANES), slice(j * LANES, (j + 1) * LANES)
                re, im = tile(p + i, p + j)
                s_re[at, to], s_im[at, to] = re - less_re[at, to], im - less_im[at, to]

    def block(p, q):
        at, to = slice(p * LANES, (p + 1) * LANES), slice(q * LANES, (q + 1) * LANES)
        e = embed(s_re[at, to], s_im[at, to])
        return e + (window if p == 0 else -window) * eye(2 * LANES) if p == q else e

    none = jnp.zeros((half, half), f32)
    load(0, none, none)

    def invert(t, _):
        i_re, i_im = quasi_inverse(block, newton)
        inv_ref[t, 0], inv_ref[t, 1] = i_re, i_im

        @pl.when(t == 0)
        def _():
            k21_re, k21_im = lines(2, 0)
            w = near(embed(i_re, i_im), jnp.concatenate([k21_re.T, -k21_im.T], 0))
            w_ref[0], w_ref[1] = w[:half], w[half:]
            fold = near(embed(k21_re, k21_im), w)
            load(2, fold[:half], fold[half:])

        return 0

    lax.fori_loop(0, 2, invert, 0)
    g_re, g_im, i_re, i_im = inv_ref[0, 0], inv_ref[0, 1], inv_ref[1, 0], inv_ref[1, 1]
    w_re, w_im = w_ref[0], w_ref[1]
    g_emb = embed(g_re, g_im)
    for copy in late:
        copy.wait()
    q1 = jnp.concatenate([q_ref[:rows, :half], q_ref[rows:, :half]], 1)
    q2 = jnp.concatenate([q_ref[:rows, half:], q_ref[rows:, half:]], 1)
    y = near(q1, embed(g_re, -g_im))
    x2 = near(q2 - near(q1, embed(w_re, -w_im)), embed(i_re, -i_im))
    x1 = y - near(x2, embed(w_re.T, w_im.T))
    x_ref[:, :half], x_ref[:, half:width] = x1[:, :half], x2[:, :half]
    x_ref[:, width : width + half], x_ref[:, width + half :] = x1[:, half:], x2[:, half:]
    dirs = h_ref.shape[1]
    b = b_ref[...] + b_more[...]
    b = jnp.concatenate([b[:, :dirs], b[:, dirs:]], 0)
    gb = near(g_emb, b)
    power_ref[...] = jnp.sum(b * gb, axis=0, keepdims=True)
    h_out[...] = h_ref[...] - near(embed(q_ref[:rows, :half], q_ref[rows:, :half]), gb)


def solve(window, kmats, bmats, local, h):
    width = local.shape[1]
    rows, dirs = h.shape[0] // 2, h.shape[1]
    return pl.pallas_call(
        lambda *refs: solve_kernel(window, *refs),
        out_shape=[
            jax.ShapeDtypeStruct((rows, 2 * width), f32),
            jax.ShapeDtypeStruct(h.shape, f32),
            jax.ShapeDtypeStruct((1, dirs), f32),
        ],
        in_specs=[pl.BlockSpec(memory_space=pltpu.VMEM)] * 2 + [pl.BlockSpec(memory_space=pl.ANY)] * 4,
        scratch_shapes=[pltpu.VMEM((width // 2, width // 2), f32)] * 2
        + [pltpu.VMEM((2 * LANES, 2 * LANES), f32)]
        + [pltpu.VMEM(lead + (width // 2, width // 2), f32) for lead in ((2, 2), (2,))]
        + [pltpu.VMEM(a.shape, f32) for a in (*bmats, local, h)]
        + [pltpu.SemaphoreType.DMA((4,))],
        compiler_params=pltpu.CompilerParams(vmem_limit_bytes=28 << 20),
        name="solve",
    )(*kmats, *bmats, local, h)


def update_kernel(plan, chip_ref, core_ref, p_ref, x_ref, h0_ref, h1_ref, scale_ref, *refs):
    out_ref, weight_ref, buf, x_high, x_low, sem = refs[-6:]
    step = pl.program_id(0)
    rows = p_ref.shape[1]
    width = x_ref.shape[1] // 2
    core = core_ref[0]

    @pl.when(step == 0)
    def _():
        high, low = split(x_ref[...])
        for ref, v in ((x_high, high), (x_low, low)):
            ref[:rows, :] = v
            ref[rows:, :width], ref[rows:, width:] = v[:, width:], -v[:, :width]

    def where(k, plane):
        return pl.multiple_of((2 * plane + (core if k == 0 else 1 - core)) * rows, rows), rows

    slot = stream(step, plan, refs, buf, sem, where)
    q_high, q_low = split(jnp.concatenate([buf[slot, : 2 * rows, :], buf[slot, 2 * rows :, :]], 1))
    part = mm_nt(x_high[...], q_high) + mm_nt(x_low[...], q_high) + mm_nt(x_high[...], q_low)
    out_ref[0] = p_ref[0] - part[:rows]
    out_ref[1] = p_ref[1] - part[rows:]
    weight_ref[0] = h0_ref[...] * scale_ref[:1, :]
    weight_ref[1] = h1_ref[...] * scale_ref[1:2, :]


def update(inverse, x, mine, theirs, chips, core, steered, scale):
    _, rows, length = inverse.shape
    width = x.shape[1] // 2
    arrays, plan = arrays_of(mine + theirs)
    count = len(mine)
    plan = [[plan[g], plan[count + g]] for g in range(count)]
    dirs = scale.shape[1]
    piece = 2 * rows // count
    return pl.pallas_call(
        lambda *refs: update_kernel(plan, *refs),
        grid_spec=pltpu.PrefetchScalarGridSpec(
            num_scalar_prefetch=2,
            grid=(count,),
            in_specs=[
                pl.BlockSpec((2, rows, 2 * rows), lambda i, s, c: (0, 0, s[i])),
                pl.BlockSpec((rows, 2 * width), lambda i, s, c: (0, 0)),
                pl.BlockSpec((piece, dirs), lambda i, s, c: (i, 0)),
                pl.BlockSpec((piece, dirs), lambda i, s, c: (i, 0)),
                pl.BlockSpec(scale.shape, lambda i, s, c: (0, 0)),
            ]
            + [pl.BlockSpec(memory_space=pl.ANY)] * len(arrays),
            out_specs=[
                pl.BlockSpec((2, rows, 2 * rows), lambda i, s, c: (0, 0, s[i])),
                pl.BlockSpec((2, piece, dirs), lambda i, s, c: (0, i, 0)),
            ],
            scratch_shapes=[
                pltpu.VMEM((2, 4 * rows, width), f32),
                pltpu.VMEM((2 * rows, 2 * width), bf16),
                pltpu.VMEM((2 * rows, 2 * width), bf16),
                pltpu.SemaphoreType.DMA((2,)),
            ],
        ),
        out_shape=[jax.ShapeDtypeStruct(inverse.shape, f32), jax.ShapeDtypeStruct((2, 2 * rows, dirs), f32)],
        compiler_params=pltpu.CompilerParams(vmem_limit_bytes=28 << 20),
        name="update",
    )(chips, core, inverse, x, *steered, scale, *arrays)


def on_device(row_count, inverse, cycle, arrivals, departing, directions):
    rows, length = inverse.shape[1], inverse.shape[2]
    window = cycle.shape[2]
    snap = arrivals.shape[3]
    dirs = directions.shape[1]
    inner = 64
    me = lax.axis_index("row").astype(jnp.int32)
    first = (me * (rows // inner))[None]
    core = (me % 2)[None]
    chips, ends = ring_chips(row_count)
    right_count, left_count = ring_counts(row_count)

    slots = departing.reshape(-1)
    pick = (jnp.arange(window, dtype=jnp.int32)[:, None] == slots[None, :]).astype(bf16)
    departed = mm(cycle.reshape(2 * rows, window), pick).astype(bf16)
    blocks = []
    for t in range(STEPS):
        blocks += [arrivals[t].reshape(2 * rows, snap), departed[:, t * snap : (t + 1) * snap]]
    own = jnp.concatenate(blocks, 1)

    tables = [steering_tables(directions[t], length, inner) for t in range(STEPS)]
    steered, powers = [], []

    def steer(after):
        after, place = together(after, first)
        return steer_product(inverse, tables[len(steered)], place)

    def travel(block, work):
        right = left = block
        for h in range(1, right_count + 1):
            held = (right, left)
            if h <= left_count:
                moved = hop(right, row_count, 1), hop(left, row_count, -1)
            elif right_count > left_count:
                moved = hop(right[:rows], row_count, 1), hop(left[rows:], row_count, -1)
            (right, left), result = together(moved, work(h, held))
            group = [whole_block(right), whole_block(left)] if h <= left_count else [((right, 0), (left, 0))]
            yield h, group, result

    mine, theirs = [whole_block(own)], [whole_block(swap(own, row_count))]
    acc, folded = None, 0

    def snaps_until(end, acc):
        return snap_product(inverse, mine[folded:end], theirs[folded:end], chips, folded, core, acc)

    def under_snaps(h, held):
        nonlocal acc, folded
        if h == 1:
            return together(tables, held)[0]
        if h == 2:
            return steer(held)
        acc, folded = snaps_until(ends[h - 1], acc), ends[h - 1]
        return acc

    for h, group, result in travel(own, under_snaps):
        if h == 1:
            tables = result
        elif h == 2:
            steered.append(result[0])
            powers.append(result[1])
        else:
            acc = result
        mine += group
        theirs += [each_array(u, lambda v: swap(v, row_count)) for u in group]
    local = snaps_until(len(mine), acc)

    sent = lax.optimization_barrier(local.astype(jnp.float16))
    wide = [whole_block(sent.astype(f32))]
    coarse, fine = tables[1][:2]
    acc, folded = None, 0
    power, stride = None, 1

    def cross_until(end, acc):
        return cross_products(mine[folded:end], wide[folded:end], chips, folded, core, coarse, fine, acc)

    def under_products(h, held):
        nonlocal acc, folded
        if h == 1:
            return steer(held)
        moved = exchange(power, stride, row_count)
        acc, folded = cross_until(ends[h - 1], acc), ends[h - 1]
        return acc, moved

    for h, group, result in travel(sent, under_products):
        if h == 1:
            steered.append(result[0])
            powers.append(result[1])
            power = jnp.concatenate(powers, 0)
            if row_count & (row_count - 1):
                power = lax.psum(power, "row")
        else:
            acc, moved = result
            power, stride = power + moved, stride * 2
        wide += [each_array(q, lambda v: v.astype(f32)) for q in group]
    moved = exchange(power, stride, row_count)
    (kmat, bmat), moved = together(cross_until(len(mine), acc), moved)
    power, stride = power + moved, stride * 2
    while stride < row_count:
        power, stride = power + exchange(power, stride, row_count), stride * 2
    kmats, bmats = (kmat, swap(kmat, row_count)), (bmat, swap(bmat, row_count))

    x, second, fold = solve(float(window), kmats, bmats, local, steered[1])
    wide_theirs = [each_array(q, lambda v: swap(v, row_count)) for q in wide]
    power = jnp.concatenate([power[:1], power[1:] - fold], 0)
    spectrum = length / power
    new_inverse, weights = update(
        inverse,
        x,
        wide,
        wide_theirs,
        chips,
        core,
        (steered[0], second),
        spectrum,
    )
    return new_inverse, weights.reshape(STEPS, 2, rows, dirs), spectrum


def solution(mesh):
    row_count = mesh.shape["row"]
    in_specs = (
        P("groups", "row", None),
        P("groups", "row", None),
        P("groups", None, "row", None),
        P("groups", None),
        P("groups", None),
    )
    out_specs = (P("groups", "row", None), P("groups", None, "row", None), P("groups", None))
    return jax.shard_map(
        lambda *args: on_device(row_count, *args), mesh=mesh, in_specs=in_specs, out_specs=out_specs, check_vma=False
    )
```
